256 devices in a mesh: tile: 16 (over y, z_hi), head: 16 (over x, z_lo, core).
Axes of the slice: x: 4, y: 4, z: 8 (z_hi: 4, z_lo: 2; z = z_hi * 2 + z_lo), core: 2. Of those that a mesh axis runs over, the one named last changes fastest.
Arguments:
- tokens: bfloat16 [6144, 3072], P('tile'), may hold values from -200 to 200
- mod_shift: float32 [3072], replicated, may hold values from -3 to 3
- mod_scale: float32 [3072], replicated, may hold values from -2.5 to 2.5
- mod_gate: float32 [3072], replicated, may hold values from -4 to 4
- qkv_weight: bfloat16 [3072, 6144], P(None, 'head'), may hold values from -1 to 1
- out_weight: bfloat16 [2048, 3072], P('head'), may hold values from -0.125 to 0.125
- teacher: bfloat16 [6144, 3072], P('tile'), may hold values from -6 to 6
- slot_tiles: int32 [16], replicated, may hold values from 0 to 15, each once
Outputs:
- qkv_grad: float32 [3072, 6144], P('tile', 'head')
- out_grad: float32 [2048, 3072], P('head', 'tile')
The draws below stay inside these ranges and needn't reach their ends.
Inputs may be any that keep to these rules, and one draw needn't show every extreme that they name: Slot s, rows s * 384 to (s + 1) * 384 - 1 of tokens and teacher, holds tile slot_tiles[s]; every tile once.
All inputs are finite; a program needn't handle non-finite values.
Results may differ from the reference program's by a relative error of at most 0.00049.
Values may be sent and summed in bfloat16 or wider, within the bound.
A program may use at most 128 MiB of HBM per device.

```python
import math
import jax
import jax.numpy as jnp
from jax import lax

D = 3072
HD = 128
TOK_TILE = 384
TH = 4
HEADS = 16
TILES = 16
TW = 4
TOKENS = 6144


def draw_tokens(key, part):
    base_key, col_key, row_key = jax.random.split(key, 3)
    col_scale = jnp.exp(jax.random.uniform(col_key, (1, D), jnp.float32, 0.0, math.log(10.0)))
    row_scale = jnp.exp(jax.random.uniform(row_key, (TOKENS, 1), jnp.float32, math.log(0.5), math.log(5.0)))
    base_values = jax.random.normal(base_key, (TOKENS, D), jnp.float32)
    return (jnp.clip(base_values, -4.0, 4.0) * col_scale * row_scale).astype(jnp.bfloat16)


def draw_qkv_weight(key, part):
    query_key, noise_key, value_key = jax.random.split(jax.random.fold_in(key, 7), 3)
    fan_scale = 1.0 / math.sqrt(D)
    query_cols = jnp.clip(jax.random.normal(query_key, (D, HEADS, 1, HD), jnp.float32), -6.0, 6.0)
    noise_cols = jnp.clip(jax.random.normal(noise_key, (D, HEADS, 1, HD), jnp.float32), -4.0, 4.0)
    value_cols = jnp.clip(jax.random.normal(value_key, (D, HEADS, 1, HD), jnp.float32), -6.0, 6.0)
    key_cols = query_cols + 0.25 * noise_cols
    joined = jnp.concatenate([query_cols, key_cols, value_cols], 2) * fan_scale
    return joined.reshape(D, HEADS * 3 * HD).astype(jnp.bfloat16)


def levels(stream_key, shape, cuts, smallest, top_value):
    loudness, own = 1.0, jax.random.fold_in(stream_key, 6)
    for axis_at, parts in cuts:
        heights = jnp.exp(jax.random.uniform(jax.random.fold_in(own, axis_at), (parts,), jnp.float32, smallest / len(cuts), top_value / len(cuts)))
        loudness = loudness * jnp.repeat(heights, shape[axis_at] // parts).reshape([-1 if axis == axis_at else 1 for axis in range(len(shape))])
    return loudness


def bell_draw(stream_key, dims, scale, limit, cuts=(), kind=jnp.bfloat16):
    gain = levels(stream_key, dims, cuts, -0.22, 0.18) if cuts else 1.0
    drawn = jax.random.normal(stream_key, dims, jnp.float32) * scale * gain
    return jnp.minimum(jnp.maximum(drawn, -limit), limit).astype(kind)


def setup_inputs(seed: int = 0) -> dict:
    seeds = jax.random.split(jax.random.key(seed), 9)
    return {
        "tokens": draw_tokens(jax.random.fold_in(seeds[8], 71), 0),
        "mod_shift": bell_draw(seeds[1], (D,), 0.5, 3.0, (), jnp.float32),
        "mod_scale": bell_draw(seeds[2], (D,), 0.5, 2.5, (), jnp.float32),
        "mod_gate": bell_draw(seeds[3], (D,), 1.0, 4.0, (), jnp.float32),
        "qkv_weight": draw_qkv_weight(jax.random.fold_in(seeds[8], 71), 0),
        "out_weight": bell_draw(seeds[5], (HEADS * HD, D), (HEADS * HD) ** -0.5, 0.125, ((0, 16),)),
        "teacher": bell_draw(seeds[6], (TOKENS, D), 1.0, 6.0, ((0, 16),)),
        "slot_tiles": jax.random.permutation(seeds[7], TILES).astype(jnp.int32),
    }


EPS_NORM = 1e-05
EPS_ROOT = 1e-06
LOSS_WEIGHT = 32.0

def root_norm(values):
    factor = lax.rsqrt(lax.optimization_barrier(jnp.mean(values * values, -1, keepdims=True)) + EPS_ROOT)
    return (values * factor, factor)

def root_norm_back(grad_unit, unit_value, factor):
    return factor * (grad_unit - unit_value * lax.optimization_barrier(jnp.mean(grad_unit * unit_value, -1, keepdims=True)))

def near_tiles(first_tiles, second_tiles, width_tiles):

    def coords(ids):
        return (ids // (TH * width_tiles), ids // width_tiles % TH, ids % width_tiles)
    ta, ha, wa = coords(first_tiles[:, None])
    tb, hb, wb = coords(second_tiles[None, :])
    close = (jnp.abs(ta - tb) <= 1) & (jnp.abs(ha - hb) <= 1) & (jnp.abs(wa - wb) <= 1)
    return close.astype(jnp.float32)

def reference(tokens, mod_shift, mod_scale, mod_gate, qkv_weight, out_weight, teacher, slot_tiles):
    att_scale = 1.0 / math.sqrt(HD)
    values_in = tokens.astype(jnp.float32)
    center = values_in - lax.optimization_barrier(jnp.mean(values_in, -1, keepdims=True))
    spread = lax.optimization_barrier(jnp.mean(center * center, -1, keepdims=True))
    normed = (center * lax.rsqrt(spread + EPS_NORM) * (1.0 + mod_scale) + mod_shift).astype(jnp.bfloat16)
    projected = jnp.dot(normed, qkv_weight, preferred_element_type=jnp.float32).reshape(TOKENS, HEADS, 3, HD)
    query_unit, query_factor = root_norm(projected[:, :, 0])
    key_unit, key_factor = root_norm(projected[:, :, 1])
    query_b = query_unit.astype(jnp.bfloat16)
    key_b = key_unit.astype(jnp.bfloat16)
    value_b = projected[:, :, 2].astype(jnp.bfloat16)
    tile_mask = near_tiles(slot_tiles, slot_tiles, TW)
    key_full = key_b.astype(jnp.float32)
    value_full = value_b.astype(jnp.float32)

    def tile_weights(tile_index):
        query_tile = lax.dynamic_slice_in_dim(query_b, tile_index * TOK_TILE, TOK_TILE, 0).astype(jnp.float32)
        scores = jnp.einsum('qhd,khd->hqk', query_tile, key_full) * att_scale
        key_mask = jnp.repeat(tile_mask[tile_index], TOK_TILE)
        exp_scores = jnp.exp(scores) * key_mask[None, None, :]
        totals = lax.optimization_barrier(jnp.sum(exp_scores, -1))
        return (query_tile, exp_scores / totals[:, :, None])

    def forward_tile(tile_index):
        query_tile, att_probs = tile_weights(tile_index)
        probs_b = lax.optimization_barrier(att_probs.astype(jnp.bfloat16)).astype(jnp.float32)
        return jnp.einsum('hqk,khd->qhd', probs_b, value_full).astype(jnp.bfloat16)
    tile_ids = jnp.arange(TILES, dtype=jnp.int32)
    attended = lax.map(forward_tile, tile_ids).reshape(TOKENS, HEADS, HD)
    flat_att = attended.reshape(TOKENS, HEADS * HD)
    branch = jnp.dot(flat_att, out_weight, preferred_element_type=jnp.float32)
    residual = LOSS_WEIGHT * (mod_gate * branch - teacher.astype(jnp.float32))
    grad_branch = (mod_gate * residual).astype(jnp.bfloat16)
    out_grad = jnp.dot(flat_att.T, grad_branch, preferred_element_type=jnp.float32)
    grad_att = jnp.dot(grad_branch, out_weight.T, preferred_element_type=jnp.float32)
    grad_att = grad_att.reshape(TOKENS, HEADS, HD).astype(jnp.bfloat16)
    row_delta = lax.optimization_barrier(jnp.sum(grad_att.astype(jnp.float32) * attended.astype(jnp.float32), -1))

    def backward_tile(running, tile_index):
        query_tile, att_probs = tile_weights(tile_index)
        grad_tile = lax.dynamic_slice_in_dim(grad_att, tile_index * TOK_TILE, TOK_TILE, 0).astype(jnp.float32)
        delta_tile = lax.dynamic_slice_in_dim(row_delta, tile_index * TOK_TILE, TOK_TILE, 0)
        grad_probs = jnp.einsum('qhd,khd->hqk', grad_tile, value_full)
        grad_scores = att_probs * (grad_probs - delta_tile.T[:, :, None])
        grad_scores = lax.optimization_barrier(grad_scores.astype(jnp.bfloat16)).astype(jnp.float32)
        probs_b = lax.optimization_barrier(att_probs.astype(jnp.bfloat16)).astype(jnp.float32)
        grad_query_tile = jnp.einsum('hqk,khd->qhd', grad_scores, key_full) * att_scale
        key_sum = running[0] + jnp.einsum('hqk,qhd->khd', grad_scores, query_tile) * att_scale
        value_sum = running[1] + jnp.einsum('hqk,qhd->khd', probs_b, grad_tile)
        return ((key_sum, value_sum), grad_query_tile)
    zero_keys = jnp.zeros((TOKENS, HEADS, HD), jnp.float32)
    (grad_key_unit, grad_value), grad_query_unit = lax.scan(backward_tile, (zero_keys, zero_keys), tile_ids)
    grad_query_unit = grad_query_unit.reshape(TOKENS, HEADS, HD)
    grad_query = root_norm_back(grad_query_unit, query_unit, query_factor)
    grad_key = root_norm_back(grad_key_unit, key_unit, key_factor)
    grad_qkv = jnp.stack([grad_query, grad_key, grad_value], 2).astype(jnp.bfloat16).reshape(TOKENS, HEADS * 3 * HD)
    qkv_grad = jnp.dot(normed.T, grad_qkv, preferred_element_type=jnp.float32)
    return (qkv_grad, out_grad)
```

```python
import functools
import math

import jax
import jax.numpy as jnp
from jax import lax
from jax.experimental import pallas as pl
from jax.experimental.pallas import tpu as pltpu
from jax.sharding import PartitionSpec as P

HD = 128
TOK_TILE = 384
TH = 4
TW = 4
SIDE = 4
EPS_NORM = 1e-05
EPS_ROOT = 1e-06
LOSS_WEIGHT = 32.0
ATT_SCALE = 1.0 / math.sqrt(HD)
BF16 = jnp.bfloat16
F32 = jnp.float32
MESH = pl.DeviceIdType.MESH
NT = (((1,), (1,)), ((), ()))
VMEM_LIMIT = 60 * 1024 * 1024


class Places:

    def __init__(self):
        self.t = lax.axis_index("tile")
        self.h = lax.axis_index("head")
        self.a = self.t // SIDE
        self.b = self.t % SIDE
        self.x = self.h // 4
        self.lo = self.h % 4

    def tile(self, j, k):
        return lax.rem(self.a + j, SIDE) * SIDE + lax.rem(self.b + k, SIDE)

    def head(self, j, flip):
        lo = self.lo
        if flip & 1:
            lo = lo + 1 - 2 * lax.rem(lo, 2)
        if flip & 2:
            lo = lax.rem(lo + 2, 4)
        return lax.rem(self.x + j, 4) * 4 + lo


TASK_SEMS = {"tag": 16, "hag": 16, "ha2a": 16, "ycols": 4, "yag": 4, "ya2a": 4, "za2a": 4}


def task_peers(kind):
    if kind == "tag":
        return {("t", 0, k) for k in (1, 2, 3)} | {("t", j, 0) for j in (1, 2, 3)}
    if kind == "hag":
        return {("h", j, 0) for j in (1, 2, 3)} | {("h", 0, 2), ("h", 0, 1)}
    if kind == "ha2a":
        return {("h", j, f) for j in range(4) for f in range(4)} - {("h", 0, 0)}
    if kind == "za2a":
        return {("t", 0, k) for k in (1, 2, 3)}
    return {("t", j, 0) for j in (1, 2, 3)}


def out_slots(kind):
    return 16 if kind in ("tag", "hag", "ha2a") else 4


def comm_kernel(kinds, *refs):
    n = len(kinds)
    ins, outs = refs[:n], refs[n : 2 * n]
    sems = refs[2 * n :]
    at = Places()

    def device(peer):
        axis, j, k = peer
        if axis == "t":
            return (at.tile(j, k), at.h)
        return (at.t, at.head(j, k))

    def back(peer):
        axis, j, k = peer
        if axis == "t":
            return ("t", (4 - j) % 4, (4 - k) % 4)
        return ("h", (4 - j) % 4, k)

    peers = sorted(set().union(*[task_peers(kind) for kind in kinds]))
    barrier = pltpu.get_barrier_semaphore()
    for peer in peers:
        pl.semaphore_signal(barrier, inc=1, device_id=device(peer), device_id_type=MESH)
    pl.semaphore_wait(barrier, len(peers))

    started = []
    locals_ = []

    def send(i, src, slot, index, peer):
        copy = pltpu.make_async_remote_copy(
            src_ref=src,
            dst_ref=outs[i].at[slot],
            send_sem=sems[3 * i].at[index],
            recv_sem=sems[3 * i + 1].at[index],
            device_id=device(peer),
            device_id_type=MESH,
        )
        copy.start()
        started.append(copy)

    def arrive(i, slot, index, peer):
        pltpu.make_async_remote_copy(
            src_ref=outs[i].at[slot],
            dst_ref=outs[i].at[slot],
            send_sem=sems[3 * i].at[index],
            recv_sem=sems[3 * i + 1].at[index],
            device_id=device(peer),
            device_id_type=MESH,
        ).wait_recv()

    def keep(i, src, slot):
        copy = pltpu.make_async_copy(src, outs[i].at[slot], sems[3 * i + 2].at[0])
        copy.start()
        locals_.append(copy)

    later = []
    for i, kind in enumerate(kinds):
        src = ins[i]
        if kind == "tag":
            for k in (1, 3, 2):
                send(i, src, at.t, k, ("t", 0, k))
            for j in (1, 3, 2):
                send(i, src, at.t, 4 * j, ("t", j, 0))
            keep(i, src, at.t)

            def forward(i=i):
                for k in (1, 3, 2):
                    slot = at.tile(0, 4 - k)
                    arrive(i, slot, k, ("t", 0, k))
                    for j in (1, 3, 2):
                        send(i, outs[i].at[slot], slot, 4 * j + k, ("t", j, 0))

            def finish(i=i):
                for k in range(4):
                    for j in (1, 3, 2):
                        arrive(i, at.tile(4 - j, 4 - k), 4 * j + k, ("t", j, 0))

            later.append((forward, finish))
        elif kind == "hag":
            send(i, src, at.h, 4, ("h", 0, 2))
            for j in (1, 3, 2):
                send(i, src, at.h, j, ("h", j, 0))
            send(i, src, at.h, 8, ("h", 0, 1))
            keep(i, src, at.h)

            def forward(i=i):
                slot = at.head(0, 2)
                arrive(i, slot, 4, ("h", 0, 2))
                for j in (1, 3, 2):
                    send(i, outs[i].at[slot], slot, 4 + j, ("h", j, 0))
                send(i, outs[i].at[slot], slot, 12, ("h", 0, 1))

            def finish(i=i):
                for z in (0, 1):
                    for j in (1, 3, 2):
                        slot = at.head(4 - j, 2 * z)
                        arrive(i, slot, 4 * z + j, ("h", j, 0))
                        send(i, outs[i].at[slot], slot, 8 + 4 * z + j, ("h", 0, 1))
                for z in (0, 1):
                    for j in range(4):
                        arrive(i, at.head(4 - j, 2 * z + 1), 8 + 4 * z + j, ("h", 0, 1))

            later.append((forward, finish))
        elif kind == "ha2a":
            for f in (3, 2, 1, 0):
                for j in range(4):
                    if f or j:
                        send(i, src.at[at.head(j, f)], at.h, 4 * f + j, ("h", j, f))
            keep(i, src.at[at.h], at.h)

            def finish(i=i):
                for f in range(4):
                    for j in range(4):
                        if f or j:
                            arrive(i, at.head(4 - j, f), 4 * f + j, ("h", j, f))

            later.append((None, finish))
        else:
            along_z = kind == "za2a"

            def spot(j):
                return lax.rem((at.b if along_z else at.a) + j, SIDE)

            def piece(j):
                if kind == "yag":
                    return src
                if kind == "ycols":
                    width = src.shape[1] // SIDE
                    return src.at[:, pl.ds(pl.multiple_of(spot(j) * width, 128), width)]
                return src.at[spot(j)]

            def peer_of(j, along_z=along_z):
                return ("t", 0, j) if along_z else ("t", j, 0)

            mine = spot(0)
            for j in (1, 3, 2):
                send(i, piece(j), mine, j, peer_of(j))
            keep(i, piece(0), mine)
            froms = {j: spot(4 - j) for j in (1, 2, 3)}

            def finish(i=i, froms=froms, peer_of=peer_of):
                for j in (1, 3, 2):
                    arrive(i, froms[j], j, peer_of(j))

            later.append((None, finish))

    for forward, _ in later:
        if forward is not None:
            forward()
    for _, finish in later:
        finish()
    for copy in started:
        copy.wait_send()
    for copy in locals_:
        copy.wait()


def exchange(name, cid, *tasks):
    kinds = tuple(kind for kind, _ in tasks)
    arrays = [array for _, array in tasks]
    shapes = []
    for kind, array in tasks:
        if kind in ("tag", "hag", "yag"):
            piece = array.shape
        elif kind == "ycols":
            piece = (array.shape[0], array.shape[1] // SIDE)
        else:
            piece = array.shape[1:]
        shapes.append(jax.ShapeDtypeStruct((out_slots(kind),) + piece, array.dtype))
    scratch = []
    for kind in kinds:
        scratch += [
            pltpu.SemaphoreType.DMA((TASK_SEMS[kind],)),
            pltpu.SemaphoreType.DMA((TASK_SEMS[kind],)),
            pltpu.SemaphoreType.DMA((1,)),
        ]
    return pl.pallas_call(
        functools.partial(comm_kernel, kinds),
        out_shape=shapes,
        in_specs=[pl.BlockSpec(memory_space=pltpu.VMEM)] * len(arrays),
        out_specs=[pl.BlockSpec(memory_space=pl.ANY)] * len(arrays),
        scratch_shapes=scratch,
        compiler_params=pltpu.CompilerParams(
            collective_id=cid, has_side_effects=True, vmem_limit_bytes=16 * 1024 * 1024
        ),
        name=name,
    )(*arrays)


def near(first, second):
    def coords(ids):
        return ids // (TH * TW), ids // TW % TH, ids % TW

    close = True
    for one, two in zip(coords(first), coords(second)):
        close = close & (jnp.abs(one - two) <= 1)
    return close


def attend_kernel(slots_ref, query_ref, kv_ref, att_ref, inv_ref, exp_ref, total_ref, acc_ref):
    mine = slots_ref[lax.axis_index("tile")]
    total_ref[...] = jnp.zeros_like(total_ref)
    acc_ref[...] = jnp.zeros_like(acc_ref)
    count = kv_ref.shape[0]

    @pl.loop(0, count)
    def _(j):
        @pl.when(near(mine, slots_ref[j]))
        def _():
            scores = lax.dot_general(
                query_ref[...], kv_ref[j, :, :HD], NT, preferred_element_type=F32
            )
            grown = jnp.exp(scores * ATT_SCALE)
            exp_ref[j] = grown
            total_ref[...] += jnp.sum(grown, -1, keepdims=True)

    inv = 1.0 / total_ref[...]
    inv_ref[...] = jnp.broadcast_to(inv, inv_ref.shape)

    @pl.loop(0, count)
    def _(j):
        @pl.when(near(mine, slots_ref[j]))
        def _():
            probs = (exp_ref[j] * inv).astype(BF16)
            acc_ref[...] += jnp.dot(probs, kv_ref[j, :, HD:], preferred_element_type=F32)

    att_ref[...] = acc_ref[...].astype(BF16)


def attend(slots, query_b, all_kv):
    rows = query_b.shape[0]
    return pl.pallas_call(
        attend_kernel,
        out_shape=(
            jax.ShapeDtypeStruct((rows, HD), BF16),
            jax.ShapeDtypeStruct((rows, HD), F32),
        ),
        in_specs=[
            pl.BlockSpec(memory_space=pltpu.SMEM),
            pl.BlockSpec(memory_space=pltpu.VMEM),
            pl.BlockSpec(memory_space=pltpu.VMEM),
        ],
        out_specs=(
            pl.BlockSpec(memory_space=pltpu.VMEM),
            pl.BlockSpec(memory_space=pltpu.VMEM),
        ),
        scratch_shapes=[
            pltpu.VMEM((all_kv.shape[0], rows, rows), F32),
            pltpu.VMEM((rows, 1), F32),
            pltpu.VMEM((rows, HD), F32),
        ],
        compiler_params=pltpu.CompilerParams(vmem_limit_bytes=VMEM_LIMIT),
        name="attend",
    )(slots, query_b, all_kv)


def branch_kernel(weight_ref, att_ref, teacher_ref, gate_ref, grad_ref):
    total = None
    for h in range(att_ref.shape[0]):
        term = lax.dot_general(weight_ref[h], att_ref[h], NT, preferred_element_type=F32)
        total = term if total is None else total + term
    gate = gate_ref[...]
    residual = LOSS_WEIGHT * (gate * total - teacher_ref[...].astype(F32))
    grad_ref[...] = (gate * residual).astype(BF16)


def branch_grad(weight_parts, att_parts, teacher_part, gate_part):
    return pl.pallas_call(
        branch_kernel,
        out_shape=jax.ShapeDtypeStruct(teacher_part.shape, BF16),
        in_specs=[pl.BlockSpec(memory_space=pltpu.VMEM)] * 4,
        out_specs=pl.BlockSpec(memory_space=pltpu.VMEM),
        compiler_params=pltpu.CompilerParams(vmem_limit_bytes=VMEM_LIMIT),
        name="branch_grad",
    )(weight_parts, att_parts, teacher_part, gate_part)


def out_kernel(grad_ref, weight_ref, att_ref, inv_ref, term_ref, gatt_ref, stats_ref, delta_ref):
    rows = att_ref.shape[0]
    step = grad_ref.shape[1]
    grad_t = jnp.zeros((HD, rows), F32)
    for h in range(grad_ref.shape[0]):
        block = grad_ref[h]
        grad_t += jnp.dot(
            weight_ref[:, h * step : (h + 1) * step], block, preferred_element_type=F32
        )
        term_ref[h // SIDE, (h % SIDE) * step : (h % SIDE + 1) * step, :] = jnp.dot(
            block, att_ref[...], preferred_element_type=F32
        )
    gatt = grad_t.T.astype(BF16)
    gatt_ref[...] = gatt
    delta = jnp.sum(gatt.astype(F32) * att_ref[...].astype(F32), -1, keepdims=True)
    delta_all = jnp.broadcast_to(delta, (rows, HD))
    delta_ref[...] = delta_all
    stats_ref[0:8, :] = inv_ref[...].T[0:8]
    stats_ref[8:16, :] = delta_all.T[0:8]


def out_grads(grad_parts, out_weight, attended, inv):
    rows = attended.shape[0]
    parts, step = grad_parts.shape[:2]
    return pl.pallas_call(
        out_kernel,
        out_shape=(
            jax.ShapeDtypeStruct((SIDE, parts // SIDE * step, HD), F32),
            jax.ShapeDtypeStruct((rows, HD), BF16),
            jax.ShapeDtypeStruct((16, rows), F32),
            jax.ShapeDtypeStruct((rows, HD), F32),
        ),
        in_specs=[pl.BlockSpec(memory_space=pltpu.VMEM)] * 4,
        out_specs=(pl.BlockSpec(memory_space=pltpu.VMEM),) * 4,
        compiler_params=pltpu.CompilerParams(vmem_limit_bytes=VMEM_LIMIT),
        name="out_grads",
    )(grad_parts, out_weight, attended, inv)


def root_back(grad_unit, values):
    factor = lax.rsqrt(jnp.mean(values * values, -1, keepdims=True) + EPS_ROOT)
    unit = values * factor
    return factor * (grad_unit - unit * jnp.mean(grad_unit * unit, -1, keepdims=True))


def back_kernel(
    slots_ref,
    proj_ref,
    query_ref,
    kv_ref,
    gatt_ref,
    stats_ref,
    inv_ref,
    delta_ref,
    out_ref,
    dq_ref,
    dk_ref,
    dv_ref,
):
    me = lax.axis_index("tile")
    mine = slots_ref[me]
    dq_ref[...] = jnp.zeros_like(dq_ref)
    dk_ref[...] = jnp.zeros_like(dk_ref)
    dv_ref[...] = jnp.zeros_like(dv_ref)
    my_inv = inv_ref[:, 0:1]
    my_delta = delta_ref[:, 0:1]

    @pl.loop(0, kv_ref.shape[0])
    def _(j):
        @pl.when(near(mine, slots_ref[j]))
        def _():
            key_j = kv_ref[j, :, :HD]
            scores = lax.dot_general(query_ref[me], key_j, NT, preferred_element_type=F32)
            probs = jnp.exp(scores * ATT_SCALE) * my_inv
            gprobs = lax.dot_general(
                gatt_ref[me], kv_ref[j, :, HD:], NT, preferred_element_type=F32
            )
            gscores = (probs * (gprobs - my_delta)).astype(BF16)
            dq_ref[...] += jnp.dot(gscores, key_j, preferred_element_type=F32)

            query_j = query_ref[j]
            gatt_j = gatt_ref[j]
            scores_t = lax.dot_general(
                kv_ref[me, :, :HD], query_j, NT, preferred_element_type=F32
            )
            probs_t = jnp.exp(scores_t * ATT_SCALE) * stats_ref[j, 0:1, :]
            dv_ref[...] += jnp.dot(probs_t.astype(BF16), gatt_j, preferred_element_type=F32)
            gprobs_t = lax.dot_general(
                kv_ref[me, :, HD:], gatt_j, NT, preferred_element_type=F32
            )
            gscores_t = (probs_t * (gprobs_t - stats_ref[j, 8:9, :])).astype(BF16)
            dk_ref[...] += jnp.dot(gscores_t, query_j, preferred_element_type=F32)

    out_ref[:, :HD] = root_back(dq_ref[...] * ATT_SCALE, proj_ref[:, :HD]).astype(BF16)
    out_ref[:, HD : 2 * HD] = root_back(
        dk_ref[...] * ATT_SCALE, proj_ref[:, HD : 2 * HD]
    ).astype(BF16)
    out_ref[:, 2 * HD :] = dv_ref[...].astype(BF16)


def attend_back(slots, projected, all_query, all_kv, all_gatt, all_stats, inv, delta):
    rows = projected.shape[0]
    return pl.pallas_call(
        back_kernel,
        out_shape=jax.ShapeDtypeStruct((rows, 3 * HD), BF16),
        in_specs=[pl.BlockSpec(memory_space=pltpu.SMEM)]
        + [pl.BlockSpec(memory_space=pltpu.VMEM)] * 7,
        out_specs=pl.BlockSpec(memory_space=pltpu.VMEM),
        scratch_shapes=[pltpu.VMEM((rows, HD), F32)] * 3,
        compiler_params=pltpu.CompilerParams(vmem_limit_bytes=VMEM_LIMIT),
        name="attend_back",
    )(slots, projected, all_query, all_kv, all_gatt, all_stats, inv, delta)


def modulated_norm(tokens, mod_shift, mod_scale):
    values_in = tokens.astype(F32)
    center = values_in - jnp.mean(values_in, -1, keepdims=True)
    spread = jnp.mean(center * center, -1, keepdims=True)
    return (center * lax.rsqrt(spread + EPS_NORM) * (1.0 + mod_scale) + mod_shift).astype(BF16)


def root_norm(values):
    return values * lax.rsqrt(jnp.mean(values * values, -1, keepdims=True) + EPS_ROOT)


def per_device(tokens, mod_shift, mod_scale, mod_gate, qkv_weight, out_weight, teacher, slot_tiles):
    width = out_weight.shape[1]
    step = width // 16
    head = lax.axis_index("head")
    normed = modulated_norm(tokens, mod_shift, mod_scale)
    projected = jnp.dot(normed, qkv_weight, preferred_element_type=F32)
    query_b = root_norm(projected[:, :HD]).astype(BF16)
    key_b = root_norm(projected[:, HD : 2 * HD]).astype(BF16)
    kv = jnp.concatenate([key_b, projected[:, 2 * HD :].astype(BF16)], 1)
    weight_t = out_weight.T.reshape(16, step, HD)
    teacher_part = lax.dynamic_slice_in_dim(teacher, head * step, step, 1).T
    gate_part = lax.dynamic_slice_in_dim(mod_gate, head * step, step, 0)[:, None]

    all_kv, weight_parts = exchange("share_kv", 1, ("tag", kv), ("ha2a", weight_t))
    attended, inv = attend(slot_tiles, query_b, all_kv)
    att_parts, all_query = exchange("share_att", 2, ("hag", attended), ("tag", query_b))
    grad_part = branch_grad(weight_parts, att_parts, teacher_part, gate_part)
    grad_parts, normed_parts = exchange("share_grad", 3, ("hag", grad_part), ("ycols", normed))
    out_term, gatt, stats, delta = out_grads(grad_parts, out_weight, attended, inv)
    all_gatt, all_stats = exchange("share_gatt", 4, ("tag", gatt), ("tag", stats))
    grad_qkv = attend_back(
        slot_tiles, projected, all_query, all_kv, all_gatt, all_stats, inv, delta
    )
    qkv_parts, out_parts = exchange("share_qkv", 5, ("yag", grad_qkv), ("ya2a", out_term))
    qkv_term = lax.dot_general(
        normed_parts.reshape(-1, width // SIDE),
        qkv_parts.reshape(-1, 3 * HD),
        (((0,), (0,)), ((), ())),
        preferred_element_type=F32,
    )
    out_sum = jnp.sum(out_parts, 0).reshape(SIDE, step, HD)
    qkv_pieces, out_pieces = exchange(
        "share_sums",
        6,
        ("za2a", qkv_term.reshape(SIDE, step, 3 * HD)),
        ("za2a", out_sum),
    )
    return (jnp.sum(qkv_pieces, 0), jnp.sum(out_pieces, 0).T)


def solution(mesh):
    return jax.shard_map(
        per_device,
        mesh=mesh,
        in_specs=(
            P("tile", None),
            P(),
            P(),
            P(),
            P(None, "head"),
            P("head", None),
            P("tile", None),
            P(),
        ),
        out_specs=(P("tile", "head"), P("head", "tile")),
        check_vma=False,
    )
```

```python
import functools
import math

import jax
import jax.numpy as jnp
from jax import lax
from jax.experimental import pallas as pl
from jax.experimental.pallas import tpu as pltpu
from jax.sharding import PartitionSpec as P

HD = 128
TOK_TILE = 384
TH = 4
TW = 4
SIDE = 4
EPS_NORM = 1e-05
EPS_ROOT = 1e-06
LOSS_WEIGHT = 32.0
ATT_SCALE = 1.0 / math.sqrt(HD)
BF16 = jnp.bfloat16
F32 = jnp.float32
MESH = pl.DeviceIdType.MESH
NT = (((1,), (1,)), ((), ()))
VMEM_LIMIT = 32 * 1024 * 1024


class Places:

    def __init__(self):
        self.t = lax.axis_index("tile")
        self.h = lax.axis_index("head")
        self.a = self.t // SIDE
        self.b = self.t % SIDE
        self.x = self.h // 4
        self.lo = self.h % 4

    def tile(self, j, k):
        return lax.rem(self.a + j, SIDE) * SIDE + lax.rem(self.b + k, SIDE)

    def head(self, j, flip):
        lo = self.lo
        if flip & 1:
            lo = lo + 1 - 2 * lax.rem(lo, 2)
        if flip & 2:
            lo = lax.rem(lo + 2, 4)
        return lax.rem(self.x + j, 4) * 4 + lo


TASK_SEMS = {"tag": 20, "hag": 18, "ha2a": 16, "ycols": 8, "yag": 5, "ya2a": 4, "za2a": 4}


def task_peers(kind):
    if kind == "tag":
        return {("t", 0, k) for k in (1, 2, 3)} | {("t", j, 0) for j in (1, 3)}
    if kind == "hag":
        return {("h", j, 0) for j in (1, 3)} | {("h", 0, 2), ("h", 0, 1)}
    if kind == "ha2a":
        return {("h", j, f) for j in range(4) for f in range(4)} - {("h", 0, 0)}
    if kind == "za2a":
        return {("t", 0, k) for k in (1, 2, 3)}
    if kind == "yag":
        return {("t", j, 0) for j in (1, 3)}
    if kind == "ycols":
        return {("t", j, 0) for j in (1, 2, 3)} | {("h", 0, 1)}
    return {("t", j, 0) for j in (1, 2, 3)}


def out_slots(kind):
    return 16 if kind in ("tag", "hag", "ha2a") else 4


def comm_kernel(kinds, *refs):
    n = len(kinds)
    ins, outs = refs[:n], refs[n : 2 * n]
    sems = refs[2 * n :]
    at = Places()

    def device(peer):
        axis, j, k = peer
        if axis == "t":
            return (at.tile(j, k), at.h)
        return (at.t, at.head(j, k))

    peers = sorted(set().union(*[task_peers(kind) for kind in kinds]))
    barrier = pltpu.get_barrier_semaphore()
    for peer in peers:
        pl.semaphore_signal(barrier, inc=1, device_id=device(peer), device_id_type=MESH)
    pl.semaphore_wait(barrier, len(peers))

    started = []
    locals_ = []

    def send(i, src, dst, index, peer):
        copy = pltpu.make_async_remote_copy(
            src_ref=src,
            dst_ref=dst,
            send_sem=sems[3 * i].at[index],
            recv_sem=sems[3 * i + 1].at[index],
            device_id=device(peer),
            device_id_type=MESH,
        )
        copy.start()
        started.append(copy)

    def arrive(i, dst, index, peer):
        pltpu.make_async_remote_copy(
            src_ref=dst,
            dst_ref=dst,
            send_sem=sems[3 * i].at[index],
            recv_sem=sems[3 * i + 1].at[index],
            device_id=device(peer),
            device_id_type=MESH,
        ).wait_recv()

    def keep(i, src, slot):
        copy = pltpu.make_async_copy(src, outs[i].at[slot], sems[3 * i + 2].at[0])
        copy.start()
        locals_.append(copy)

    steps = []
    for i, kind in enumerate(kinds):
        src = ins[i]
        out = outs[i]

        def half(slot, part, out=out):
            rows = out.shape[1] // 2
            return out.at[slot, pl.ds(part * rows, rows)]

        if kind in ("tag", "hag", "yag"):
            unit = math.prod(src.shape) * src.dtype.itemsize / 45000.0
            axis = "h" if kind == "hag" else "t"

            def slot_of(j, k, kind=kind):
                if kind == "hag":
                    return at.head(j, 2 * k)
                if kind == "tag":
                    return at.tile(j, k)
                return lax.rem(at.a + j, SIDE)

            def spread(i, k, block, axis=axis, slot_of=slot_of, out=out):
                slot = slot_of(0, 4 - k if axis == "t" and k else k)
                for j in (1, 3):
                    send(i, block, out.at[slot], 4 * j + k, (axis, j, 0))

            def relay(i, k, axis=axis, slot_of=slot_of, half=half, out=out, kind=kind):
                back = 4 - k if axis == "t" and k else k
                for j, part in ((1, 0), (3, 1)):
                    slot = slot_of(4 - j, back)
                    arrive(i, out.at[slot], 4 * j + k, (axis, j, 0))
                    send(i, half(slot, part), half(slot, part), (8 + k, k)[part], (axis, j, 0))
                    if kind == "hag":
                        send(i, out.at[slot], out.at[slot], (4 * j + 2 + k), ("h", 0, 1))

            def far(i, k, axis=axis, slot_of=slot_of, half=half, out=out, kind=kind):
                back = 4 - k if axis == "t" and k else k
                slot = slot_of(2, back)
                arrive(i, half(slot, 0), 8 + k, (axis, 1, 0))
                arrive(i, half(slot, 1), k, (axis, 3, 0))
                if kind == "hag":
                    send(i, out.at[slot], out.at[slot], 10 + k, ("h", 0, 1))

            if kind == "tag":
                for k in (1, 3, 2):
                    send(i, src, out.at[at.t], 15 + k + (k == 1) * 3, ("t", 0, k))
                spread(i, 0, src)
                keep(i, src, at.t)

                def onward(i=i, out=out, spread=spread, ks=()):
                    for k in ks:
                        slot = at.tile(0, 4 - k)
                        arrive(i, out.at[slot], 15 + k + (k == 1) * 3, ("t", 0, k))
                        spread(i, k, out.at[slot])

                steps.append((unit + 1, functools.partial(relay, i, 0)))
                steps.append((2 * unit + 1, functools.partial(onward, ks=(1, 3))))
                steps.append((3 * unit + 1, functools.partial(relay, i, 1)))
                steps.append((4 * unit + 1, functools.partial(relay, i, 3)))
                steps.append((4.5 * unit + 1, functools.partial(onward, ks=(2,))))
                steps.append((6 * unit + 1, functools.partial(relay, i, 2)))
                for k in (0, 1, 3, 2):
                    steps.append((1000, functools.partial(far, i, k)))
            elif kind == "hag":
                send(i, src, out.at[at.h], 16, ("h", 0, 2))
                spread(i, 0, src)
                send(i, src, out.at[at.h], 2, ("h", 0, 1))
                keep(i, src, at.h)

                def onward(i=i, out=out, spread=spread):
                    slot = at.head(0, 2)
                    arrive(i, out.at[slot], 16, ("h", 0, 2))
                    spread(i, 1, out.at[slot])
                    send(i, out.at[slot], out.at[slot], 3, ("h", 0, 1))

                def finish(i=i, out=out):
                    for k in (0, 1):
                        for j in range(4):
                            slot = at.head(4 - j, 2 * k + 1)
                            arrive(i, out.at[slot], 4 * j + 2 + k, ("h", 0, 1))

                steps.append((unit, onward))
                steps.append((unit + 1, functools.partial(relay, i, 0)))
                steps.append((2 * unit + 1, functools.partial(relay, i, 1)))
                for k in (0, 1):
                    steps.append(((2.5 + k) * unit + 1, functools.partial(far, i, k)))
                steps.append((1001, finish))
            else:
                for j in (1, 3):
                    send(i, src, out.at[at.a], j, ("t", j, 0))
                keep(i, src, at.a)

                def pass_on(i=i, half=half, out=out):
                    for j, part in ((1, 0), (3, 1)):
                        slot = lax.rem(at.a + 4 - j, SIDE)
                        arrive(i, out.at[slot], j, ("t", j, 0))
                        send(i, half(slot, part), half(slot, part), (2, 4)[part], ("t", j, 0))

                def finish(i=i, half=half):
                    slot = lax.rem(at.a + 2, SIDE)
                    arrive(i, half(slot, 0), 2, ("t", 1, 0))
                    arrive(i, half(slot, 1), 4, ("t", 3, 0))

                steps.append((unit + 1, pass_on))
                steps.append((1000, finish))
        elif kind == "ha2a":
            for f in (3, 2, 1, 0):
                for j in range(4):
                    if f or j:
                        send(i, src.at[at.head(j, f)], out.at[at.h], 4 * f + j, ("h", j, f))
            keep(i, src.at[at.h], at.h)

            def finish(i=i, out=out):
                for f in range(4):
                    for j in range(4):
                        if f or j:
                            arrive(i, out.at[at.head(4 - j, f)], 4 * f + j, ("h", j, f))

            steps.append((1000, finish))
        elif kind == "ycols":
            width = src.shape[1] // SIDE
            rows = src.shape[0] // 2
            mine = pl.ds(pl.multiple_of(lax.rem(at.h, 2) * rows, rows), rows)
            other = pl.ds(pl.multiple_of((1 - lax.rem(at.h, 2)) * rows, rows), rows)

            def columns(j, width=width):
                return pl.ds(pl.multiple_of(lax.rem(at.a + j, SIDE) * width, 128), width)

            for j in (2, 1, 3):
                send(i, src.at[mine, columns(j)], out.at[at.a, mine], j, ("t", j, 0))
            keep(i, src.at[:, columns(0)], at.a)

            def share(i=i, out=out, mine=mine):
                for j in (1, 3, 2):
                    block = out.at[lax.rem(at.a + 4 - j, SIDE), mine]
                    arrive(i, block, j, ("t", j, 0))
                    send(i, block, block, 4 + j, ("h", 0, 1))

            def finish(i=i, out=out, other=other):
                for j in (1, 3, 2):
                    block = out.at[lax.rem(at.a + 4 - j, SIDE), other]
                    arrive(i, block, 4 + j, ("h", 0, 1))

            steps.append((999, share))
            steps.append((1002, finish))
        else:
            along_z = kind == "za2a"

            def spot(j, along_z=along_z):
                return lax.rem((at.b if along_z else at.a) + j, SIDE)

            def peer_of(j, along_z=along_z):
                return ("t", 0, j) if along_z else ("t", j, 0)

            for j in (1, 3, 2):
                send(i, src.at[spot(j)], out.at[spot(0)], j, peer_of(j))
            keep(i, src.at[spot(0)], spot(0))

            def finish(i=i, out=out, spot=spot, peer_of=peer_of):
                for j in (1, 3, 2):
                    arrive(i, out.at[spot(4 - j)], j, peer_of(j))

            steps.append((1000, finish))

    for _, step in sorted(steps, key=lambda step: step[0]):
        step()
    for copy in started:
        copy.wait_send()
    for copy in locals_:
        copy.wait()


def exchange(name, cid, *tasks):
    kinds = tuple(kind for kind, _ in tasks)
    arrays = [array for _, array in tasks]
    shapes = []
    for kind, array in tasks:
        if kind in ("tag", "hag", "yag"):
            piece = array.shape
        elif kind == "ycols":
            piece = (array.shape[0], array.shape[1] // SIDE)
        else:
            piece = array.shape[1:]
        shapes.append(jax.ShapeDtypeStruct((out_slots(kind),) + piece, array.dtype))
    scratch = []
    for kind in kinds:
        scratch += [
            pltpu.SemaphoreType.DMA((TASK_SEMS[kind],)),
            pltpu.SemaphoreType.DMA((TASK_SEMS[kind],)),
            pltpu.SemaphoreType.DMA((1,)),
        ]
    return pl.pallas_call(
        functools.partial(comm_kernel, kinds),
        out_shape=shapes,
        in_specs=[pl.BlockSpec(memory_space=pltpu.VMEM)] * len(arrays),
        out_specs=[pl.BlockSpec(memory_space=pltpu.VMEM)] * len(arrays),
        scratch_shapes=scratch,
        compiler_params=pltpu.CompilerParams(
            collective_id=cid, has_side_effects=True, vmem_limit_bytes=16 * 1024 * 1024
        ),
        name=name,
    )(*arrays)


def near(first, second):
    def coords(ids):
        return ids // (TH * TW), ids // TW % TH, ids % TW

    close = True
    for one, two in zip(coords(first), coords(second)):
        close = close & (jnp.abs(one - two) <= 1)
    return close


def attend_kernel(slots_ref, query_ref, kv_ref, att_ref, inv_ref, exp_ref, total_ref, acc_ref):
    mine = slots_ref[lax.axis_index("tile")]
    total_ref[...] = jnp.zeros_like(total_ref)
    acc_ref[...] = jnp.zeros_like(acc_ref)
    count = kv_ref.shape[0]

    @pl.loop(0, count)
    def _(j):
        @pl.when(near(mine, slots_ref[j]))
        def _():
            scores = lax.dot_general(
                query_ref[...], kv_ref[j, :, :HD], NT, preferred_element_type=F32
            )
            grown = jnp.exp(scores * ATT_SCALE)
            exp_ref[j] = grown
            total_ref[...] += jnp.sum(grown, -1, keepdims=True)

    inv = 1.0 / total_ref[...]
    inv_ref[...] = jnp.broadcast_to(inv, inv_ref.shape)

    @pl.loop(0, count)
    def _(j):
        @pl.when(near(mine, slots_ref[j]))
        def _():
            probs = (exp_ref[j] * inv).astype(BF16)
            acc_ref[...] += jnp.dot(probs, kv_ref[j, :, HD:], preferred_element_type=F32)

    att_ref[...] = acc_ref[...].astype(BF16)


def attend(slots, query_b, all_kv):
    rows = query_b.shape[0]
    return pl.pallas_call(
        attend_kernel,
        out_shape=(
            jax.ShapeDtypeStruct((rows, HD), BF16),
            jax.ShapeDtypeStruct((rows, HD), F32),
        ),
        in_specs=[
            pl.BlockSpec(memory_space=pltpu.SMEM),
            pl.BlockSpec(memory_space=pltpu.VMEM),
            pl.BlockSpec(memory_space=pltpu.VMEM),
        ],
        out_specs=(
            pl.BlockSpec(memory_space=pltpu.VMEM),
            pl.BlockSpec(memory_space=pltpu.VMEM),
        ),
        scratch_shapes=[
            pltpu.VMEM((all_kv.shape[0], rows, rows), F32),
            pltpu.VMEM((rows, 1), F32),
            pltpu.VMEM((rows, HD), F32),
        ],
        compiler_params=pltpu.CompilerParams(vmem_limit_bytes=VMEM_LIMIT),
        name="attend",
    )(slots, query_b, all_kv)


def branch_kernel(weight_ref, att_ref, teacher_ref, gate_ref, grad_ref):
    total = None
    for h in range(att_ref.shape[0]):
        term = lax.dot_general(weight_ref[h], att_ref[h], NT, preferred_element_type=F32)
        total = term if total is None else total + term
    gate = gate_ref[...]
    residual = LOSS_WEIGHT * (gate * total - teacher_ref[...].astype(F32))
    grad_ref[...] = (gate * residual).astype(BF16)


def branch_grad(weight_parts, att_parts, teacher_part, gate_part):
    return pl.pallas_call(
        branch_kernel,
        out_shape=jax.ShapeDtypeStruct(teacher_part.shape, BF16),
        in_specs=[pl.BlockSpec(memory_space=pltpu.VMEM)] * 4,
        out_specs=pl.BlockSpec(memory_space=pltpu.VMEM),
        compiler_params=pltpu.CompilerParams(vmem_limit_bytes=VMEM_LIMIT),
        name="branch_grad",
    )(weight_parts, att_parts, teacher_part, gate_part)


def out_kernel(grad_ref, weight_ref, att_ref, inv_ref, term_ref, gatt_ref, stats_ref, delta_ref):
    rows = att_ref.shape[0]
    step = grad_ref.shape[1]
    grad_t = jnp.zeros((HD, rows), F32)
    for h in range(grad_ref.shape[0]):
        block = grad_ref[h]
        grad_t += jnp.dot(
            weight_ref[:, h * step : (h + 1) * step], block, preferred_element_type=F32
        )
        term_ref[h // SIDE, (h % SIDE) * step : (h % SIDE + 1) * step, :] = jnp.dot(
            block, att_ref[...], preferred_element_type=F32
        )
    gatt = grad_t.T.astype(BF16)
    gatt_ref[...] = gatt
    delta = jnp.sum(gatt.astype(F32) * att_ref[...].astype(F32), -1, keepdims=True)
    delta_all = jnp.broadcast_to(delta, (rows, HD))
    delta_ref[...] = delta_all
    stats_ref[0:8, :] = inv_ref[...].T[0:8]
    stats_ref[8:16, :] = delta_all.T[0:8]


def out_grads(grad_parts, out_weight, attended, inv):
    rows = attended.shape[0]
    parts, step = grad_parts.shape[:2]
    return pl.pallas_call(
        out_kernel,
        out_shape=(
            jax.ShapeDtypeStruct((SIDE, parts // SIDE * step, HD), F32),
            jax.ShapeDtypeStruct((rows, HD), BF16),
            jax.ShapeDtypeStruct((16, rows), F32),
            jax.ShapeDtypeStruct((rows, HD), F32),
        ),
        in_specs=[pl.BlockSpec(memory_space=pltpu.VMEM)] * 4,
        out_specs=(pl.BlockSpec(memory_space=pltpu.VMEM),) * 4,
        compiler_params=pltpu.CompilerParams(vmem_limit_bytes=VMEM_LIMIT),
        name="out_grads",
    )(grad_parts, out_weight, attended, inv)


def root_back(grad_unit, values):
    factor = lax.rsqrt(jnp.mean(values * values, -1, keepdims=True) + EPS_ROOT)
    unit = values * factor
    return factor * (grad_unit - unit * jnp.mean(grad_unit * unit, -1, keepdims=True))


def back_kernel(
    slots_ref,
    proj_ref,
    query_ref,
    kv_ref,
    gatt_ref,
    stats_ref,
    inv_ref,
    delta_ref,
    out_ref,
    dq_ref,
    dk_ref,
    dv_ref,
):
    me = lax.axis_index("tile")
    mine = slots_ref[me]
    dq_ref[...] = jnp.zeros_like(dq_ref)
    dk_ref[...] = jnp.zeros_like(dk_ref)
    dv_ref[...] = jnp.zeros_like(dv_ref)
    my_inv = inv_ref[:, 0:1]
    my_delta = delta_ref[:, 0:1]

    @pl.loop(0, kv_ref.shape[0])
    def _(j):
        @pl.when(near(mine, slots_ref[j]))
        def _():
            key_j = kv_ref[j, :, :HD]
            scores = lax.dot_general(query_ref[me], key_j, NT, preferred_element_type=F32)
            probs = jnp.exp(scores * ATT_SCALE) * my_inv
            gprobs = lax.dot_general(
                gatt_ref[me], kv_ref[j, :, HD:], NT, preferred_element_type=F32
            )
            gscores = (probs * (gprobs - my_delta)).astype(BF16)
            dq_ref[...] += jnp.dot(gscores, key_j, preferred_element_type=F32)

            query_j = query_ref[j]
            gatt_j = gatt_ref[j]
            scores_t = lax.dot_general(
                kv_ref[me, :, :HD], query_j, NT, preferred_element_type=F32
            )
            probs_t = jnp.exp(scores_t * ATT_SCALE) * stats_ref[j, 0:1, :]
            dv_ref[...] += jnp.dot(probs_t.astype(BF16), gatt_j, preferred_element_type=F32)
            gprobs_t = lax.dot_general(
                kv_ref[me, :, HD:], gatt_j, NT, preferred_element_type=F32
            )
            gscores_t = (probs_t * (gprobs_t - stats_ref[j, 8:9, :])).astype(BF16)
            dk_ref[...] += jnp.dot(gscores_t, query_j, preferred_element_type=F32)

    out_ref[:, :HD] = root_back(dq_ref[...] * ATT_SCALE, proj_ref[:, :HD]).astype(BF16)
    out_ref[:, HD : 2 * HD] = root_back(
        dk_ref[...] * ATT_SCALE, proj_ref[:, HD : 2 * HD]
    ).astype(BF16)
    out_ref[:, 2 * HD :] = dv_ref[...].astype(BF16)


def attend_back(slots, projected, all_query, all_kv, all_gatt, all_stats, inv, delta):
    rows = projected.shape[0]
    return pl.pallas_call(
        back_kernel,
        out_shape=jax.ShapeDtypeStruct((rows, 3 * HD), BF16),
        in_specs=[pl.BlockSpec(memory_space=pltpu.SMEM)]
        + [pl.BlockSpec(memory_space=pltpu.VMEM)] * 7,
        out_specs=pl.BlockSpec(memory_space=pltpu.VMEM),
        scratch_shapes=[pltpu.VMEM((rows, HD), F32)] * 3,
        compiler_params=pltpu.CompilerParams(vmem_limit_bytes=VMEM_LIMIT),
        name="attend_back",
    )(slots, projected, all_query, all_kv, all_gatt, all_stats, inv, delta)


def modulated_norm(tokens, mod_shift, mod_scale):
    values_in = tokens.astype(F32)
    center = values_in - jnp.mean(values_in, -1, keepdims=True)
    spread = jnp.mean(center * center, -1, keepdims=True)
    return (center * lax.rsqrt(spread + EPS_NORM) * (1.0 + mod_scale) + mod_shift).astype(BF16)


def root_norm(values):
    return values * lax.rsqrt(jnp.mean(values * values, -1, keepdims=True) + EPS_ROOT)


def per_device(tokens, mod_shift, mod_scale, mod_gate, qkv_weight, out_weight, teacher, slot_tiles):
    width = out_weight.shape[1]
    step = width // 16
    head = lax.axis_index("head")
    normed = modulated_norm(tokens, mod_shift, mod_scale)
    projected = jnp.dot(normed, qkv_weight, preferred_element_type=F32)
    query_b = root_norm(projected[:, :HD]).astype(BF16)
    key_b = root_norm(projected[:, HD : 2 * HD]).astype(BF16)
    kv = jnp.concatenate([key_b, projected[:, 2 * HD :].astype(BF16)], 1)
    weight_t = out_weight.T.reshape(16, step, HD)
    teacher_part = lax.dynamic_slice_in_dim(teacher, head * step, step, 1).T
    gate_part = lax.dynamic_slice_in_dim(mod_gate, head * step, step, 0)[:, None]

    all_kv, weight_parts = exchange("share_kv", 1, ("tag", kv), ("ha2a", weight_t))
    attended, inv = attend(slot_tiles, query_b, all_kv)
    att_parts, all_query = exchange("share_att", 2, ("hag", attended), ("tag", query_b))
    grad_part = branch_grad(weight_parts, att_parts, teacher_part, gate_part)
    grad_parts, normed_parts = exchange("share_grad", 3, ("hag", grad_part), ("ycols", normed))
    out_term, gatt, stats, delta = out_grads(grad_parts, out_weight, attended, inv)
    all_gatt, all_stats = exchange("share_gatt", 4, ("tag", gatt), ("tag", stats))
    grad_qkv = attend_back(
        slot_tiles, projected, all_query, all_kv, all_gatt, all_stats, inv, delta
    )
    qkv_parts, out_parts = exchange("share_qkv", 5, ("yag", grad_qkv), ("ya2a", out_term))
    qkv_term = lax.dot_general(
        normed_parts.reshape(-1, width // SIDE),
        qkv_parts.reshape(-1, 3 * HD),
        (((0,), (0,)), ((), ())),
        preferred_element_type=F32,
    )
    out_sum = jnp.sum(out_parts, 0).reshape(SIDE, step, HD)
    qkv_pieces, out_pieces = exchange(
        "share_sums",
        6,
        ("za2a", qkv_term.reshape(SIDE, step, 3 * HD)),
        ("za2a", out_sum),
    )
    return (jnp.sum(qkv_pieces, 0), jnp.sum(out_pieces, 0).T)


def solution(mesh):
    return jax.shard_map(
        per_device,
        mesh=mesh,
        in_specs=(
            P("tile", None),
            P(),
            P(),
            P(),
            P(None, "head"),
            P("head", None),
            P("tile", None),
            P(),
        ),
        out_specs=(P("tile", "head"), P("head", "tile")),
        check_vma=False,
    )
```

```python
import functools
import math

import jax
import jax.numpy as jnp
from jax import lax
from jax.experimental import pallas as pl
from jax.experimental.pallas import tpu as pltpu
from jax.sharding import PartitionSpec as P

HD = 128
TOK_TILE = 384
TH = 4
TW = 4
SIDE = 4
EPS_NORM = 1e-05
EPS_ROOT = 1e-06
LOSS_WEIGHT = 32.0
ATT_SCALE = 1.0 / math.sqrt(HD)
BF16 = jnp.bfloat16
F32 = jnp.float32
MESH = pl.DeviceIdType.MESH
NT = (((1,), (1,)), ((), ()))
VMEM_LIMIT = 24 * 1024 * 1024
COMM_LIMIT = 8 * 1024 * 1024


class Places:

    def __init__(self):
        self.t = lax.axis_index("tile")
        self.h = lax.axis_index("head")
        self.a = self.t // SIDE
        self.b = self.t % SIDE
        self.x = self.h // 4
        self.lo = self.h % 4

    def tile(self, j, k):
        return lax.rem(self.a + j, SIDE) * SIDE + lax.rem(self.b + k, SIDE)

    def head(self, j, flip):
        lo = self.lo
        if flip & 1:
            lo = lo + 1 - 2 * lax.rem(lo, 2)
        if flip & 2:
            lo = lax.rem(lo + 2, 4)
        return lax.rem(self.x + j, 4) * 4 + lo


TASK_SEMS = {"tag": 20, "hag": 18, "ha2a": 16, "ycols": 8, "yag": 5, "ya2a": 4, "za2a": 4}


def task_peers(kind):
    if kind == "tag":
        return {("t", 0, 1), ("t", 0, 3), ("t", 1, 0), ("t", 3, 0)}
    if kind == "hag":
        return {("h", j, 0) for j in (1, 3)} | {("h", 0, 2), ("h", 0, 1)}
    if kind == "ha2a":
        return {("h", j, f) for j in range(4) for f in range(4)} - {("h", 0, 0)}
    if kind == "za2a":
        return {("t", 0, k) for k in (1, 2, 3)}
    if kind == "yag":
        return {("t", j, 0) for j in (1, 3)}
    if kind == "ycols":
        return {("t", j, 0) for j in (1, 2, 3)} | {("h", 0, 1)}
    return {("t", j, 0) for j in (1, 2, 3)}


def out_slots(kind):
    return 16 if kind in ("tag", "hag", "ha2a") else 4


def comm_kernel(kinds, *refs):
    n = len(kinds)
    ins, outs = refs[:n], refs[n : 2 * n]
    sems = refs[2 * n :]
    at = Places()

    def device(peer):
        axis, j, k = peer
        if axis == "t":
            return (at.tile(j, k), at.h)
        return (at.t, at.head(j, k))

    peers = sorted(set().union(*[task_peers(kind) for kind in kinds]))
    barrier = pltpu.get_barrier_semaphore()
    for peer in peers:
        pl.semaphore_signal(barrier, inc=1, device_id=device(peer), device_id_type=MESH)
    pl.semaphore_wait(barrier, len(peers))

    started = []
    locals_ = []

    def send(i, src, dst, index, peer):
        copy = pltpu.make_async_remote_copy(
            src_ref=src,
            dst_ref=dst,
            send_sem=sems[3 * i].at[index],
            recv_sem=sems[3 * i + 1].at[index],
            device_id=device(peer),
            device_id_type=MESH,
        )
        copy.start()
        started.append(copy)

    def arrive(i, dst, index, peer):
        pltpu.make_async_remote_copy(
            src_ref=dst,
            dst_ref=dst,
            send_sem=sems[3 * i].at[index],
            recv_sem=sems[3 * i + 1].at[index],
            device_id=device(peer),
            device_id_type=MESH,
        ).wait_recv()

    def keep(i, src, slot):
        copy = pltpu.make_async_copy(src, outs[i].at[slot], sems[3 * i + 2].at[0])
        copy.start()
        locals_.append(copy)

    steps = []
    for i, kind in enumerate(kinds):
        src = ins[i]
        out = outs[i]

        def half(slot, part, out=out):
            rows = out.shape[1] // 2
            if rows < 8:
                return out.at[slot, :, pl.ds(*((0, 256), (256, out.shape[2] - 256))[part])]
            return out.at[slot, pl.ds(part * rows, rows)]

        if kind in ("tag", "hag", "yag"):
            axis = "h" if kind == "hag" else "t"

            def slot_of(j, k, kind=kind):
                if kind == "hag":
                    return at.head(j, 2 * k)
                if kind == "tag":
                    return at.tile(j, k)
                return lax.rem(at.a + j, SIDE)

            def spread(i, k, block, axis=axis, slot_of=slot_of, out=out):
                slot = slot_of(0, 4 - k if axis == "t" and k else k)
                for j in (1, 3):
                    send(i, block, out.at[slot], 4 * j + k, (axis, j, 0))

            def relay(i, k, axis=axis, slot_of=slot_of, half=half, out=out, kind=kind):
                back = 4 - k if axis == "t" and k else k
                for j, part in ((1, 0), (3, 1)):
                    slot = slot_of(4 - j, back)
                    arrive(i, out.at[slot], 4 * j + k, (axis, j, 0))
                    send(i, half(slot, part), half(slot, part), (8 + k, k)[part], (axis, j, 0))
                    if kind == "hag":
                        send(i, out.at[slot], out.at[slot], (4 * j + 2 + k), ("h", 0, 1))

            def far(i, k, axis=axis, slot_of=slot_of, half=half, out=out, kind=kind):
                back = 4 - k if axis == "t" and k else k
                slot = slot_of(2, back)
                arrive(i, half(slot, 0), 8 + k, (axis, 1, 0))
                arrive(i, half(slot, 1), k, (axis, 3, 0))
                if kind == "hag":
                    send(i, out.at[slot], out.at[slot], 10 + k, ("h", 0, 1))

            if kind == "tag":
                for k in (1, 3):
                    send(i, src, out.at[at.t], 16 + k, ("t", 0, k))
                spread(i, 0, src)
                keep(i, src, at.t)

                def onward(i=i, out=out, spread=spread, half=half):
                    for k, part in ((1, 0), (3, 1)):
                        slot = at.tile(0, 4 - k)
                        arrive(i, out.at[slot], 16 + k, ("t", 0, k))
                        piece = half(slot, part)
                        send(i, piece, piece, (16, 18)[part], ("t", 0, k))
                        spread(i, k, out.at[slot])

                def last(i=i, out=out, spread=spread, half=half):
                    slot = at.tile(0, 2)
                    arrive(i, half(slot, 0), 16, ("t", 0, 1))
                    arrive(i, half(slot, 1), 18, ("t", 0, 3))
                    spread(i, 2, out.at[slot])

                steps.append((2, functools.partial(relay, i, 0)))
                steps.append((3, onward))
                steps.append((4.5, functools.partial(relay, i, 1)))
                steps.append((5, last))
                steps.append((5.5, functools.partial(relay, i, 3)))
                steps.append((7, functools.partial(relay, i, 2)))
                for k in (0, 1, 3, 2):
                    steps.append((1000, functools.partial(far, i, k)))
            elif kind == "hag":
                send(i, src, out.at[at.h], 16, ("h", 0, 2))
                spread(i, 0, src)
                send(i, src, out.at[at.h], 2, ("h", 0, 1))
                keep(i, src, at.h)

                def onward(i=i, out=out, spread=spread):
                    slot = at.head(0, 2)
                    arrive(i, out.at[slot], 16, ("h", 0, 2))
                    spread(i, 1, out.at[slot])
                    send(i, out.at[slot], out.at[slot], 3, ("h", 0, 1))

                def finish(i=i, out=out):
                    for k in (0, 1):
                        for j in range(4):
                            slot = at.head(4 - j, 2 * k + 1)
                            arrive(i, out.at[slot], 4 * j + 2 + k, ("h", 0, 1))

                steps.append((1, onward))
                steps.append((1.5, functools.partial(relay, i, 0)))
                steps.append((3.2, functools.partial(relay, i, 1)))
                steps.append((4, functools.partial(far, i, 0)))
                steps.append((5.2, functools.partial(far, i, 1)))
                steps.append((1001, finish))
            else:
                for j in (1, 3):
                    send(i, src, out.at[at.a], j, ("t", j, 0))
                keep(i, src, at.a)

                def pass_on(i=i, half=half, out=out):
                    for j, part in ((1, 0), (3, 1)):
                        slot = lax.rem(at.a + 4 - j, SIDE)
                        arrive(i, out.at[slot], j, ("t", j, 0))
                        send(i, half(slot, part), half(slot, part), (2, 4)[part], ("t", j, 0))

                def finish(i=i, half=half):
                    slot = lax.rem(at.a + 2, SIDE)
                    arrive(i, half(slot, 0), 2, ("t", 1, 0))
                    arrive(i, half(slot, 1), 4, ("t", 3, 0))

                steps.append((1, pass_on))
                steps.append((1000, finish))
        elif kind == "ha2a":
            def give(i=i, src=src, out=out, flips=()):
                for f in flips:
                    for j in range(4):
                        if f or j:
                            send(i, src.at[at.head(j, f)], out.at[at.h], 4 * f + j, ("h", j, f))

            give(flips=(1, 0))
            keep(i, src.at[at.h], at.h)
            steps.append((5, functools.partial(give, flips=(3, 2))))

            def finish(i=i, out=out):
                for f in range(4):
                    for j in range(4):
                        if f or j:
                            arrive(i, out.at[at.head(4 - j, f)], 4 * f + j, ("h", j, f))

            steps.append((1000, finish))
        elif kind == "ycols":
            width = src.shape[1] // SIDE
            rows = src.shape[0] // 2
            mine = pl.ds(pl.multiple_of(lax.rem(at.h, 2) * rows, rows), rows)
            other = pl.ds(pl.multiple_of((1 - lax.rem(at.h, 2)) * rows, rows), rows)

            def columns(j, width=width):
                return pl.ds(pl.multiple_of(lax.rem(at.a + j, SIDE) * width, 128), width)

            for j in (2, 1, 3):
                send(i, src.at[mine, columns(j)], out.at[at.a, mine], j, ("t", j, 0))
            keep(i, src.at[:, columns(0)], at.a)

            def share(i=i, out=out, mine=mine):
                for j in (1, 3, 2):
                    block = out.at[lax.rem(at.a + 4 - j, SIDE), mine]
                    arrive(i, block, j, ("t", j, 0))
                    send(i, block, block, 4 + j, ("h", 0, 1))

            def finish(i=i, out=out, other=other):
                for j in (1, 3, 2):
                    block = out.at[lax.rem(at.a + 4 - j, SIDE), other]
                    arrive(i, block, 4 + j, ("h", 0, 1))

            steps.append((999, share))
            steps.append((1002, finish))
        else:
            along_z = kind == "za2a"

            def spot(j, along_z=along_z):
                return lax.rem((at.b if along_z else at.a) + j, SIDE)

            def peer_of(j, along_z=along_z):
                return ("t", 0, j) if along_z else ("t", j, 0)

            for j in (1, 3, 2):
                send(i, src.at[spot(j)], out.at[spot(0)], j, peer_of(j))
            keep(i, src.at[spot(0)], spot(0))

            def finish(i=i, out=out, spot=spot, peer_of=peer_of):
                for j in (1, 3, 2):
                    arrive(i, out.at[spot(4 - j)], j, peer_of(j))

            steps.append((1000, finish))

    for _, step in sorted(steps, key=lambda step: step[0]):
        step()
    for copy in started:
        copy.wait_send()
    for copy in locals_:
        copy.wait()


def exchange(name, cid, *tasks):
    kinds = tuple(kind for kind, _ in tasks)
    arrays = [array for _, array in tasks]
    shapes = []
    for kind, array in tasks:
        if kind in ("tag", "hag", "yag"):
            piece = array.shape
        elif kind == "ycols":
            piece = (array.shape[0], array.shape[1] // SIDE)
        else:
            piece = array.shape[1:]
        shapes.append(jax.ShapeDtypeStruct((out_slots(kind),) + piece, array.dtype))
    scratch = []
    for kind in kinds:
        scratch += [
            pltpu.SemaphoreType.DMA((TASK_SEMS[kind],)),
            pltpu.SemaphoreType.DMA((TASK_SEMS[kind],)),
            pltpu.SemaphoreType.DMA((1,)),
        ]
    return pl.pallas_call(
        functools.partial(comm_kernel, kinds),
        out_shape=shapes,
        in_specs=[pl.BlockSpec(memory_space=pltpu.VMEM)] * len(arrays),
        out_specs=[pl.BlockSpec(memory_space=pltpu.VMEM)] * len(arrays),
        scratch_shapes=scratch,
        compiler_params=pltpu.CompilerParams(
            collective_id=cid, has_side_effects=True, vmem_limit_bytes=COMM_LIMIT
        ),
        name=name,
    )(*arrays)


def near(first, second):
    def coords(ids):
        return ids // (TH * TW), ids // TW % TH, ids % TW

    close = True
    for one, two in zip(coords(first), coords(second)):
        close = close & (jnp.abs(one - two) <= 1)
    return close


def attend_kernel(slots_ref, query_ref, kv_ref, att_ref, inv_ref, exp_ref, total_ref, acc_ref):
    mine = slots_ref[lax.axis_index("tile")]
    total_ref[...] = jnp.zeros_like(total_ref)
    acc_ref[...] = jnp.zeros_like(acc_ref)
    count = kv_ref.shape[0]

    @pl.loop(0, count)
    def _(j):
        @pl.when(near(mine, slots_ref[j]))
        def _():
            scores = lax.dot_general(
                query_ref[...], kv_ref[j, :, :HD], NT, preferred_element_type=F32
            )
            grown = jnp.exp(scores * ATT_SCALE)
            exp_ref[j] = grown
            total_ref[...] += jnp.sum(grown, -1, keepdims=True)

    inv = 1.0 / total_ref[...]
    inv_ref[...] = jnp.broadcast_to(inv, inv_ref.shape)

    @pl.loop(0, count)
    def _(j):
        @pl.when(near(mine, slots_ref[j]))
        def _():
            probs = (exp_ref[j] * inv).astype(BF16)
            acc_ref[...] += jnp.dot(probs, kv_ref[j, :, HD:], preferred_element_type=F32)

    att_ref[...] = acc_ref[...].astype(BF16)


def attend(slots, query_b, all_kv):
    rows = query_b.shape[0]
    return pl.pallas_call(
        attend_kernel,
        out_shape=(
            jax.ShapeDtypeStruct((rows, HD), BF16),
            jax.ShapeDtypeStruct((rows, HD), F32),
        ),
        in_specs=[
            pl.BlockSpec(memory_space=pltpu.SMEM),
            pl.BlockSpec(memory_space=pltpu.VMEM),
            pl.BlockSpec(memory_space=pltpu.VMEM),
        ],
        out_specs=(
            pl.BlockSpec(memory_space=pltpu.VMEM),
            pl.BlockSpec(memory_space=pltpu.VMEM),
        ),
        scratch_shapes=[
            pltpu.VMEM((all_kv.shape[0], rows, rows), F32),
            pltpu.VMEM((rows, 1), F32),
            pltpu.VMEM((rows, HD), F32),
        ],
        compiler_params=pltpu.CompilerParams(vmem_limit_bytes=VMEM_LIMIT),
        name="attend",
    )(slots, query_b, all_kv)


def branch_kernel(weight_ref, att_ref, teacher_ref, gate_ref, grad_ref):
    total = None
    for h in range(att_ref.shape[0]):
        term = lax.dot_general(weight_ref[h], att_ref[h], NT, preferred_element_type=F32)
        total = term if total is None else total + term
    gate = gate_ref[...]
    residual = LOSS_WEIGHT * (gate * total - teacher_ref[...].astype(F32))
    grad_ref[...] = (gate * residual).astype(BF16)


def branch_grad(weight_parts, att_parts, teacher_part, gate_part):
    return pl.pallas_call(
        branch_kernel,
        out_shape=jax.ShapeDtypeStruct(teacher_part.shape, BF16),
        in_specs=[pl.BlockSpec(memory_space=pltpu.VMEM)] * 4,
        out_specs=pl.BlockSpec(memory_space=pltpu.VMEM),
        compiler_params=pltpu.CompilerParams(vmem_limit_bytes=VMEM_LIMIT),
        name="branch_grad",
    )(weight_parts, att_parts, teacher_part, gate_part)


def out_kernel(
    grad_ref,
    weight_ref,
    att_ref,
    inv_ref,
    yterm_ref,
    zterm_ref,
    gatt_ref,
    stats_ref,
    delta_ref,
):
    rows = att_ref.shape[0]
    step = grad_ref.shape[1]
    half = step // 2
    grad_t = jnp.zeros((HD, rows), F32)
    for h in range(grad_ref.shape[0]):
        block = grad_ref[h]
        grad_t += jnp.dot(
            weight_ref[:, h * step : (h + 1) * step], block, preferred_element_type=F32
        )
        term = jnp.dot(block, att_ref[...], preferred_element_type=F32)
        low = h % SIDE * half
        yterm_ref[h // SIDE, low : low + half, :] = term[:half]
        low = h // SIDE * half
        zterm_ref[h % SIDE, low : low + half, :] = term[half:]
    gatt = grad_t.T.astype(BF16)
    gatt_ref[...] = gatt
    delta = jnp.sum(gatt.astype(F32) * att_ref[...].astype(F32), -1, keepdims=True)
    delta_all = jnp.broadcast_to(delta, (rows, HD))
    delta_ref[...] = delta_all
    stats_ref[0:4, :] = inv_ref[...].T[0:4]
    stats_ref[4:8, :] = delta_all.T[0:4]


def out_grads(grad_parts, out_weight, attended, inv):
    rows = attended.shape[0]
    parts, step = grad_parts.shape[:2]
    return pl.pallas_call(
        out_kernel,
        out_shape=(
            jax.ShapeDtypeStruct((SIDE, parts // SIDE * step // 2, HD), F32),
            jax.ShapeDtypeStruct((SIDE, parts // SIDE * step // 2, HD), F32),
            jax.ShapeDtypeStruct((rows, HD), BF16),
            jax.ShapeDtypeStruct((8, rows), F32),
            jax.ShapeDtypeStruct((rows, HD), F32),
        ),
        in_specs=[pl.BlockSpec(memory_space=pltpu.VMEM)] * 4,
        out_specs=(pl.BlockSpec(memory_space=pltpu.VMEM),) * 5,
        compiler_params=pltpu.CompilerParams(vmem_limit_bytes=VMEM_LIMIT),
        name="out_grads",
    )(grad_parts, out_weight, attended, inv)


def root_back(grad_unit, values):
    factor = lax.rsqrt(jnp.mean(values * values, -1, keepdims=True) + EPS_ROOT)
    unit = values * factor
    return factor * (grad_unit - unit * jnp.mean(grad_unit * unit, -1, keepdims=True))


def back_kernel(
    slots_ref,
    proj_ref,
    query_ref,
    kv_ref,
    gatt_ref,
    stats_ref,
    inv_ref,
    delta_ref,
    out_ref,
    dq_ref,
    dk_ref,
    dv_ref,
):
    me = lax.axis_index("tile")
    mine = slots_ref[me]
    dq_ref[...] = jnp.zeros_like(dq_ref)
    dk_ref[...] = jnp.zeros_like(dk_ref)
    dv_ref[...] = jnp.zeros_like(dv_ref)
    my_inv = inv_ref[:, 0:1]
    my_delta = delta_ref[:, 0:1]

    @pl.loop(0, kv_ref.shape[0])
    def _(j):
        @pl.when(near(mine, slots_ref[j]))
        def _():
            key_j = kv_ref[j, :, :HD]
            scores = lax.dot_general(query_ref[me], key_j, NT, preferred_element_type=F32)
            probs = jnp.exp(scores * ATT_SCALE) * my_inv
            gprobs = lax.dot_general(
                gatt_ref[me], kv_ref[j, :, HD:], NT, preferred_element_type=F32
            )
            gscores = (probs * (gprobs - my_delta)).astype(BF16)
            dq_ref[...] += jnp.dot(gscores, key_j, preferred_element_type=F32)

            query_j = query_ref[j]
            gatt_j = gatt_ref[j]
            scores_t = lax.dot_general(
                kv_ref[me, :, :HD], query_j, NT, preferred_element_type=F32
            )
            probs_t = jnp.exp(scores_t * ATT_SCALE) * stats_ref[j, 0:1, :]
            dv_ref[...] += jnp.dot(probs_t.astype(BF16), gatt_j, preferred_element_type=F32)
            gprobs_t = lax.dot_general(
                kv_ref[me, :, HD:], gatt_j, NT, preferred_element_type=F32
            )
            gscores_t = (probs_t * (gprobs_t - stats_ref[j, 4:5, :])).astype(BF16)
            dk_ref[...] += jnp.dot(gscores_t, query_j, preferred_element_type=F32)

    out_ref[:, :HD] = root_back(dq_ref[...] * ATT_SCALE, proj_ref[:, :HD]).astype(BF16)
    out_ref[:, HD : 2 * HD] = root_back(
        dk_ref[...] * ATT_SCALE, proj_ref[:, HD : 2 * HD]
    ).astype(BF16)
    out_ref[:, 2 * HD :] = dv_ref[...].astype(BF16)


def attend_back(slots, projected, all_query, all_kv, all_gatt, all_stats, inv, delta):
    rows = projected.shape[0]
    return pl.pallas_call(
        back_kernel,
        out_shape=jax.ShapeDtypeStruct((rows, 3 * HD), BF16),
        in_specs=[pl.BlockSpec(memory_space=pltpu.SMEM)]
        + [pl.BlockSpec(memory_space=pltpu.VMEM)] * 7,
        out_specs=pl.BlockSpec(memory_space=pltpu.VMEM),
        scratch_shapes=[pltpu.VMEM((rows, HD), F32)] * 3,
        compiler_params=pltpu.CompilerParams(vmem_limit_bytes=VMEM_LIMIT),
        name="attend_back",
    )(slots, projected, all_query, all_kv, all_gatt, all_stats, inv, delta)


def terms_kernel(normed_ref, grad_ref, yparts_ref, zparts_ref, qkv_ref, ysum_ref, zsum_ref):
    step = qkv_ref.shape[1]
    for k in range(qkv_ref.shape[0]):
        total = None
        for j in range(normed_ref.shape[0]):
            term = lax.dot_general(
                normed_ref[j, :, k * step : (k + 1) * step],
                grad_ref[j],
                (((0,), (0,)), ((), ())),
                preferred_element_type=F32,
            )
            total = term if total is None else total + term
        qkv_ref[k] = total
    for parts_ref, sum_ref in ((yparts_ref, ysum_ref), (zparts_ref, zsum_ref)):
        half = sum_ref.shape[1]
        for k in range(sum_ref.shape[0]):
            rows = slice(k * half, (k + 1) * half)
            sum_ref[k] = (parts_ref[0, rows] + parts_ref[1, rows]) + (
                parts_ref[2, rows] + parts_ref[3, rows]
            )


def grad_terms(normed_parts, qkv_parts, yparts, zparts):
    step = normed_parts.shape[2] // SIDE
    half = yparts.shape[1] // SIDE
    return pl.pallas_call(
        terms_kernel,
        out_shape=(
            jax.ShapeDtypeStruct((SIDE, step, 3 * HD), F32),
            jax.ShapeDtypeStruct((SIDE, half, HD), F32),
            jax.ShapeDtypeStruct((SIDE, half, HD), F32),
        ),
        in_specs=[pl.BlockSpec(memory_space=pltpu.VMEM)] * 4,
        out_specs=(pl.BlockSpec(memory_space=pltpu.VMEM),) * 3,
        compiler_params=pltpu.CompilerParams(vmem_limit_bytes=VMEM_LIMIT),
        name="grad_terms",
    )(normed_parts, qkv_parts, yparts, zparts)


def sums_kernel(qkv_ref, first_ref, second_ref, qkv_out_ref, out_out_ref):
    qkv_out_ref[...] = (qkv_ref[0] + qkv_ref[1]) + (qkv_ref[2] + qkv_ref[3])
    first = (first_ref[0] + first_ref[1]) + (first_ref[2] + first_ref[3])
    second = (second_ref[0] + second_ref[1]) + (second_ref[2] + second_ref[3])
    half = first.shape[0]
    out_out_ref[:half, :] = first
    out_out_ref[half:, :] = second


def final_sums(qkv_pieces, first, second):
    step = qkv_pieces.shape[1]
    return pl.pallas_call(
        sums_kernel,
        out_shape=(
            jax.ShapeDtypeStruct((step, 3 * HD), F32),
            jax.ShapeDtypeStruct((step, HD), F32),
        ),
        in_specs=[pl.BlockSpec(memory_space=pltpu.VMEM)] * 3,
        out_specs=(pl.BlockSpec(memory_space=pltpu.VMEM),) * 2,
        compiler_params=pltpu.CompilerParams(vmem_limit_bytes=VMEM_LIMIT),
        name="final_sums",
    )(qkv_pieces, first, second)


def modulated_norm(tokens, mod_shift, mod_scale):
    values_in = tokens.astype(F32)
    center = values_in - jnp.mean(values_in, -1, keepdims=True)
    spread = jnp.mean(center * center, -1, keepdims=True)
    return (center * lax.rsqrt(spread + EPS_NORM) * (1.0 + mod_scale) + mod_shift).astype(BF16)


def root_norm(values):
    return values * lax.rsqrt(jnp.mean(values * values, -1, keepdims=True) + EPS_ROOT)


def per_device(tokens, mod_shift, mod_scale, mod_gate, qkv_weight, out_weight, teacher, slot_tiles):
    width = out_weight.shape[1]
    step = width // 16
    head = lax.axis_index("head")
    normed = modulated_norm(tokens, mod_shift, mod_scale)
    projected = jnp.dot(normed, qkv_weight, preferred_element_type=F32)
    query_b = root_norm(projected[:, :HD]).astype(BF16)
    key_b = root_norm(projected[:, HD : 2 * HD]).astype(BF16)
    kv = jnp.concatenate([key_b, projected[:, 2 * HD :].astype(BF16)], 1)
    weight_t = out_weight.T.reshape(16, step, HD)
    teacher_part = lax.dynamic_slice_in_dim(teacher, head * step, step, 1).T
    gate_part = lax.dynamic_slice_in_dim(mod_gate, head * step, step, 0)[:, None]

    all_kv, weight_parts = exchange("share_kv", 1, ("tag", kv), ("ha2a", weight_t))
    attended, inv = attend(slot_tiles, query_b, all_kv)
    att_parts, all_query = exchange("share_att", 2, ("hag", attended), ("tag", query_b))
    grad_part = branch_grad(weight_parts, att_parts, teacher_part, gate_part)
    grad_parts, normed_parts = exchange("share_grad", 3, ("hag", grad_part), ("ycols", normed))
    yterm, zterm, gatt, stats, delta = out_grads(grad_parts, out_weight, attended, inv)
    all_gatt, all_stats = exchange("share_gatt", 4, ("tag", gatt), ("tag", stats))
    grad_qkv = attend_back(
        slot_tiles, projected, all_query, all_kv, all_gatt, all_stats, inv, delta
    )
    qkv_parts, yparts, zparts = exchange(
        "share_qkv", 5, ("yag", grad_qkv), ("ya2a", yterm), ("za2a", zterm)
    )
    qkv_term, ysum, zsum = grad_terms(normed_parts, qkv_parts, yparts, zparts)
    qkv_grad, out_grad = final_sums(
        *exchange("share_sums", 6, ("za2a", qkv_term), ("za2a", ysum), ("ya2a", zsum))
    )
    return qkv_grad, out_grad.T


def solution(mesh):
    return jax.shard_map(
        per_device,
        mesh=mesh,
        in_specs=(
            P("tile", None),
            P(),
            P(),
            P(),
            P(None, "head"),
            P("head", None),
            P("tile", None),
            P(),
        ),
        out_specs=(P("tile", "head"), P("head", "tile")),
        check_vma=False,
    )
```

```python
import functools
import math

import jax
import jax.numpy as jnp
from jax import lax
from jax.experimental import pallas as pl
from jax.experimental.pallas import tpu as pltpu
from jax.sharding import PartitionSpec as P

HD = 128
TOK_TILE = 384
TH = 4
TW = 4
SIDE = 4
EPS_NORM = 1e-05
EPS_ROOT = 1e-06
LOSS_WEIGHT = 32.0
ATT_SCALE = 1.0 / math.sqrt(HD)
BF16 = jnp.bfloat16
F32 = jnp.float32
MESH = pl.DeviceIdType.MESH
NT = (((1,), (1,)), ((), ()))
VMEM_LIMIT = 24 * 1024 * 1024
COMM_LIMIT = 8 * 1024 * 1024


class Places:

    def __init__(self):
        self.t = lax.axis_index("tile")
        self.h = lax.axis_index("head")
        self.a = self.t // SIDE
        self.b = self.t % SIDE
        self.x = self.h // 4
        self.lo = self.h % 4

    def tile(self, j, k):
        return lax.rem(self.a + j, SIDE) * SIDE + lax.rem(self.b + k, SIDE)

    def head(self, j, flip):
        lo = self.lo
        if flip & 1:
            lo = lo + 1 - 2 * lax.rem(lo, 2)
        if flip & 2:
            lo = lax.rem(lo + 2, 4)
        return lax.rem(self.x + j, 4) * 4 + lo


TASK_SEMS = {"tag": 20, "hag": 18, "ha2a": 16, "ycols": 8, "yag": 5, "yrs": 6, "zrs": 6}


def task_peers(kind):
    if kind == "tag":
        return {("t", 0, 1), ("t", 0, 3), ("t", 1, 0), ("t", 3, 0)}
    if kind == "hag":
        return {("h", j, 0) for j in (1, 3)} | {("h", 0, 2), ("h", 0, 1)}
    if kind == "ha2a":
        return {("h", j, f) for j in range(4) for f in range(4)} - {("h", 0, 0)}
    if kind == "zrs":
        return {("t", 0, k) for k in (1, 3)}
    if kind in ("yag", "yrs"):
        return {("t", j, 0) for j in (1, 3)}
    if kind == "ycols":
        return {("t", j, 0) for j in (1, 2, 3)} | {("h", 0, 1)}
    raise ValueError(kind)


def out_slots(kind):
    if kind in ("yrs", "zrs"):
        return 3
    return 16 if kind in ("tag", "hag", "ha2a") else 4


def comm_kernel(kinds, *refs):
    n = len(kinds)
    ins, outs = refs[:n], refs[n : 2 * n]
    sems = refs[2 * n : 5 * n]
    holds = list(refs[5 * n :])
    at = Places()

    def device(peer):
        axis, j, k = peer
        if axis == "t":
            return (at.tile(j, k), at.h)
        return (at.t, at.head(j, k))

    peers = sorted(set().union(*[task_peers(kind) for kind in kinds]))
    barrier = pltpu.get_barrier_semaphore()
    for peer in peers:
        pl.semaphore_signal(barrier, inc=1, device_id=device(peer), device_id_type=MESH)
    pl.semaphore_wait(barrier, len(peers))

    started = []
    locals_ = []

    def send(i, src, dst, index, peer):
        copy = pltpu.make_async_remote_copy(
            src_ref=src,
            dst_ref=dst,
            send_sem=sems[3 * i].at[index],
            recv_sem=sems[3 * i + 1].at[index],
            device_id=device(peer),
            device_id_type=MESH,
        )
        copy.start()
        started.append(copy)

    def arrive(i, dst, index, peer):
        pltpu.make_async_remote_copy(
            src_ref=dst,
            dst_ref=dst,
            send_sem=sems[3 * i].at[index],
            recv_sem=sems[3 * i + 1].at[index],
            device_id=device(peer),
            device_id_type=MESH,
        ).wait_recv()

    def keep(i, src, slot):
        copy = pltpu.make_async_copy(src, outs[i].at[slot], sems[3 * i + 2].at[0])
        copy.start()
        locals_.append(copy)

    steps = []
    for i, kind in enumerate(kinds):
        src = ins[i]
        out = outs[i]

        def half(slot, part, out=out):
            rows = out.shape[1] // 2
            if rows < 8:
                return out.at[slot, :, pl.ds(*((0, 256), (256, out.shape[2] - 256))[part])]
            return out.at[slot, pl.ds(part * rows, rows)]

        if kind in ("tag", "hag", "yag"):
            axis = "h" if kind == "hag" else "t"

            def slot_of(j, k, kind=kind):
                if kind == "hag":
                    return at.head(j, 2 * k)
                if kind == "tag":
                    return at.tile(j, k)
                return lax.rem(at.a + j, SIDE)

            def spread(i, k, block, axis=axis, slot_of=slot_of, out=out):
                slot = slot_of(0, 4 - k if axis == "t" and k else k)
                for j in (1, 3):
                    send(i, block, out.at[slot], 4 * j + k, (axis, j, 0))

            def relay(i, k, axis=axis, slot_of=slot_of, half=half, out=out, kind=kind):
                back = 4 - k if axis == "t" and k else k
                for j, part in ((1, 0), (3, 1)):
                    slot = slot_of(4 - j, back)
                    arrive(i, out.at[slot], 4 * j + k, (axis, j, 0))
                    send(i, half(slot, part), half(slot, part), (8 + k, k)[part], (axis, j, 0))
                    if kind == "hag":
                        send(i, out.at[slot], out.at[slot], (4 * j + 2 + k), ("h", 0, 1))

            def far(i, k, axis=axis, slot_of=slot_of, half=half, out=out, kind=kind):
                back = 4 - k if axis == "t" and k else k
                slot = slot_of(2, back)
                arrive(i, half(slot, 0), 8 + k, (axis, 1, 0))
                arrive(i, half(slot, 1), k, (axis, 3, 0))
                if kind == "hag":
                    send(i, out.at[slot], out.at[slot], 10 + k, ("h", 0, 1))

            if kind == "tag":
                for k in (1, 3):
                    send(i, src, out.at[at.t], 16 + k, ("t", 0, k))
                spread(i, 0, src)
                keep(i, src, at.t)

                def onward(i=i, out=out, spread=spread, half=half):
                    for k, part in ((1, 0), (3, 1)):
                        slot = at.tile(0, 4 - k)
                        arrive(i, out.at[slot], 16 + k, ("t", 0, k))
                        piece = half(slot, part)
                        send(i, piece, piece, (16, 18)[part], ("t", 0, k))
                        spread(i, k, out.at[slot])

                def last(i=i, out=out, spread=spread, half=half):
                    slot = at.tile(0, 2)
                    arrive(i, half(slot, 0), 16, ("t", 0, 1))
                    arrive(i, half(slot, 1), 18, ("t", 0, 3))
                    spread(i, 2, out.at[slot])

                steps.append((2, functools.partial(relay, i, 0)))
                steps.append((3, onward))
                steps.append((4.5, functools.partial(relay, i, 1)))
                steps.append((5, last))
                steps.append((5.5, functools.partial(relay, i, 3)))
                steps.append((7, functools.partial(relay, i, 2)))
                for k in (0, 1, 3, 2):
                    steps.append((1000, functools.partial(far, i, k)))
            elif kind == "hag":
                send(i, src, out.at[at.h], 16, ("h", 0, 2))
                spread(i, 0, src)
                send(i, src, out.at[at.h], 2, ("h", 0, 1))
                keep(i, src, at.h)

                def onward(i=i, out=out, spread=spread):
                    slot = at.head(0, 2)
                    arrive(i, out.at[slot], 16, ("h", 0, 2))
                    spread(i, 1, out.at[slot])
                    send(i, out.at[slot], out.at[slot], 3, ("h", 0, 1))

                def finish(i=i, out=out):
                    for k in (0, 1):
                        for j in range(4):
                            slot = at.head(4 - j, 2 * k + 1)
                            arrive(i, out.at[slot], 4 * j + 2 + k, ("h", 0, 1))

                steps.append((1, onward))
                steps.append((1.5, functools.partial(relay, i, 0)))
                steps.append((3.2, functools.partial(relay, i, 1)))
                steps.append((4, functools.partial(far, i, 0)))
                steps.append((5.2, functools.partial(far, i, 1)))
                steps.append((1001, finish))
            else:
                for j in (1, 3):
                    send(i, src, out.at[at.a], j, ("t", j, 0))
                keep(i, src, at.a)

                def pass_on(i=i, half=half, out=out):
                    for j, part in ((1, 0), (3, 1)):
                        slot = lax.rem(at.a + 4 - j, SIDE)
                        arrive(i, out.at[slot], j, ("t", j, 0))
                        send(i, half(slot, part), half(slot, part), (2, 4)[part], ("t", j, 0))

                def finish(i=i, half=half):
                    slot = lax.rem(at.a + 2, SIDE)
                    arrive(i, half(slot, 0), 2, ("t", 1, 0))
                    arrive(i, half(slot, 1), 4, ("t", 3, 0))

                steps.append((1, pass_on))
                steps.append((1000, finish))
        elif kind == "ha2a":
            def give(i=i, src=src, out=out, flips=()):
                for f in flips:
                    for j in range(4):
                        if f or j:
                            send(i, src.at[at.head(j, f)], out.at[at.h], 4 * f + j, ("h", j, f))

            give(flips=(1, 0))
            keep(i, src.at[at.h], at.h)
            steps.append((5, functools.partial(give, flips=(3, 2))))

            def finish(i=i, out=out):
                for f in range(4):
                    for j in range(4):
                        if f or j:
                            arrive(i, out.at[at.head(4 - j, f)], 4 * f + j, ("h", j, f))

            steps.append((1000, finish))
        elif kind == "ycols":
            width = src.shape[1] // SIDE
            rows = src.shape[0] // 2
            mine = pl.ds(pl.multiple_of(lax.rem(at.h, 2) * rows, rows), rows)
            other = pl.ds(pl.multiple_of((1 - lax.rem(at.h, 2)) * rows, rows), rows)

            def columns(j, width=width):
                return pl.ds(pl.multiple_of(lax.rem(at.a + j, SIDE) * width, 128), width)

            for j in (2, 1, 3):
                send(i, src.at[mine, columns(j)], out.at[at.a, mine], j, ("t", j, 0))
            keep(i, src.at[:, columns(0)], at.a)

            def share(i=i, out=out, mine=mine):
                for j in (1, 3, 2):
                    block = out.at[lax.rem(at.a + 4 - j, SIDE), mine]
                    arrive(i, block, j, ("t", j, 0))
                    send(i, block, block, 4 + j, ("h", 0, 1))

            def finish(i=i, out=out, other=other):
                for j in (1, 3, 2):
                    block = out.at[lax.rem(at.a + 4 - j, SIDE), other]
                    arrive(i, block, 4 + j, ("h", 0, 1))

            steps.append((999, share))
            steps.append((1002, finish))
        else:
            along_z = kind == "zrs"
            held, summed = holds.pop(0), holds.pop(0)

            def spot(j, along_z=along_z):
                return lax.rem((at.b if along_z else at.a) + j, SIDE)

            def peer_of(j, along_z=along_z):
                return ("t", 0, j) if along_z else ("t", j, 0)

            rows = src.shape[1] // 2
            parts = (pl.ds(0, rows), pl.ds(rows, rows))
            for part, j in ((0, 1), (1, 3)):
                send(i, src.at[spot(2), parts[part]], held.at[part], part, peer_of(j))
            for part, j in ((0, 1), (1, 3)):
                rest = parts[1 - part]
                send(i, src.at[spot(j), rest], out.at[1 + part, rest], 2 + part, peer_of(j))
            keep(i, src.at[spot(0)], 0)

            def add(
                i=i, src=src, out=out, held=held, summed=summed, spot=spot, peer_of=peer_of, parts=parts
            ):
                for part, j in ((0, 1), (1, 3)):
                    arrive(i, held.at[part], part, peer_of(j))
                    summed[part] = src[spot(j), parts[part], :] + held[part]
                for part, j in ((0, 1), (1, 3)):
                    send(i, summed.at[part], out.at[1 + part, parts[part]], 4 + part, peer_of(j))

            def finish(i=i, out=out, peer_of=peer_of, parts=parts):
                for part, j in ((0, 1), (1, 3)):
                    arrive(i, out.at[1 + part, parts[1 - part]], 2 + part, peer_of(j))
                    arrive(i, out.at[1 + part, parts[part]], 4 + part, peer_of(j))

            steps.append((2, add))
            steps.append((1000, finish))

    for _, step in sorted(steps, key=lambda step: step[0]):
        step()
    for copy in started:
        copy.wait_send()
    for copy in locals_:
        copy.wait()


def exchange(name, cid, *tasks):
    kinds = tuple(kind for kind, _ in tasks)
    arrays = [array for _, array in tasks]
    shapes = []
    for kind, array in tasks:
        if kind in ("tag", "hag", "yag"):
            piece = array.shape
        elif kind == "ycols":
            piece = (array.shape[0], array.shape[1] // SIDE)
        else:
            piece = array.shape[1:]
        shapes.append(jax.ShapeDtypeStruct((out_slots(kind),) + piece, array.dtype))
    scratch = []
    for kind in kinds:
        scratch += [
            pltpu.SemaphoreType.DMA((TASK_SEMS[kind],)),
            pltpu.SemaphoreType.DMA((TASK_SEMS[kind],)),
            pltpu.SemaphoreType.DMA((1,)),
        ]
    for kind, array in tasks:
        if kind in ("yrs", "zrs"):
            piece = (2, array.shape[1] // 2) + array.shape[2:]
            scratch += [pltpu.VMEM(piece, array.dtype)] * 2
    return pl.pallas_call(
        functools.partial(comm_kernel, kinds),
        out_shape=shapes,
        in_specs=[pl.BlockSpec(memory_space=pltpu.VMEM)] * len(arrays),
        out_specs=[pl.BlockSpec(memory_space=pltpu.VMEM)] * len(arrays),
        scratch_shapes=scratch,
        compiler_params=pltpu.CompilerParams(
            collective_id=cid, has_side_effects=True, vmem_limit_bytes=COMM_LIMIT
        ),
        name=name,
    )(*arrays)


def near(first, second):
    def coords(ids):
        return ids // (TH * TW), ids // TW % TH, ids % TW

    close = True
    for one, two in zip(coords(first), coords(second)):
        close = close & (jnp.abs(one - two) <= 1)
    return close


def attend_kernel(slots_ref, query_ref, kv_ref, att_ref, inv_ref, exp_ref, total_ref, acc_ref):
    mine = slots_ref[lax.axis_index("tile")]
    total_ref[...] = jnp.zeros_like(total_ref)
    acc_ref[...] = jnp.zeros_like(acc_ref)
    count = kv_ref.shape[0]

    @pl.loop(0, count)
    def _(j):
        @pl.when(near(mine, slots_ref[j]))
        def _():
            scores = lax.dot_general(
                query_ref[...], kv_ref[j, :, :HD], NT, preferred_element_type=F32
            )
            grown = jnp.exp(scores * ATT_SCALE)
            exp_ref[j] = grown
            total_ref[...] += jnp.sum(grown, -1, keepdims=True)

    inv = 1.0 / total_ref[...]
    inv_ref[...] = jnp.broadcast_to(inv, inv_ref.shape)

    @pl.loop(0, count)
    def _(j):
        @pl.when(near(mine, slots_ref[j]))
        def _():
            probs = (exp_ref[j] * inv).astype(BF16)
            acc_ref[...] += jnp.dot(probs, kv_ref[j, :, HD:], preferred_element_type=F32)

    att_ref[...] = acc_ref[...].astype(BF16)


def attend(slots, query_b, all_kv):
    rows = query_b.shape[0]
    return pl.pallas_call(
        attend_kernel,
        out_shape=(
            jax.ShapeDtypeStruct((rows, HD), BF16),
            jax.ShapeDtypeStruct((rows, HD), F32),
        ),
        in_specs=[
            pl.BlockSpec(memory_space=pltpu.SMEM),
            pl.BlockSpec(memory_space=pltpu.VMEM),
            pl.BlockSpec(memory_space=pltpu.VMEM),
        ],
        out_specs=(
            pl.BlockSpec(memory_space=pltpu.VMEM),
            pl.BlockSpec(memory_space=pltpu.VMEM),
        ),
        scratch_shapes=[
            pltpu.VMEM((all_kv.shape[0], rows, rows), F32),
            pltpu.VMEM((rows, 1), F32),
            pltpu.VMEM((rows, HD), F32),
        ],
        compiler_params=pltpu.CompilerParams(vmem_limit_bytes=VMEM_LIMIT),
        name="attend",
    )(slots, query_b, all_kv)


def branch_kernel(weight_ref, att_ref, teacher_ref, gate_ref, grad_ref):
    total = None
    for h in range(att_ref.shape[0]):
        term = lax.dot_general(weight_ref[h], att_ref[h], NT, preferred_element_type=F32)
        total = term if total is None else total + term
    gate = gate_ref[...]
    residual = LOSS_WEIGHT * (gate * total - teacher_ref[...].astype(F32))
    grad_ref[...] = (gate * residual).astype(BF16)


def branch_grad(weight_parts, att_parts, teacher_part, gate_part):
    return pl.pallas_call(
        branch_kernel,
        out_shape=jax.ShapeDtypeStruct(teacher_part.shape, BF16),
        in_specs=[pl.BlockSpec(memory_space=pltpu.VMEM)] * 4,
        out_specs=pl.BlockSpec(memory_space=pltpu.VMEM),
        compiler_params=pltpu.CompilerParams(vmem_limit_bytes=VMEM_LIMIT),
        name="branch_grad",
    )(weight_parts, att_parts, teacher_part, gate_part)


def out_kernel(
    grad_ref,
    weight_ref,
    att_ref,
    inv_ref,
    yterm_ref,
    zterm_ref,
    gatt_ref,
    stats_ref,
    delta_ref,
):
    rows = att_ref.shape[0]
    step = grad_ref.shape[1]
    half = step // 2
    grad_t = jnp.zeros((HD, rows), F32)
    for h in range(grad_ref.shape[0]):
        block = grad_ref[h]
        grad_t += jnp.dot(
            weight_ref[:, h * step : (h + 1) * step], block, preferred_element_type=F32
        )
        term = jnp.dot(block, att_ref[...], preferred_element_type=F32)
        low = h % SIDE * half
        yterm_ref[h // SIDE, low : low + half, :] = term[:half]
        low = h // SIDE * half
        zterm_ref[h % SIDE, low : low + half, :] = term[half:]
    gatt = grad_t.T.astype(BF16)
    gatt_ref[...] = gatt
    delta = jnp.sum(gatt.astype(F32) * att_ref[...].astype(F32), -1, keepdims=True)
    delta_all = jnp.broadcast_to(delta, (rows, HD))
    delta_ref[...] = delta_all
    stats_ref[0:4, :] = inv_ref[...].T[0:4]
    stats_ref[4:8, :] = delta_all.T[0:4]


def out_grads(grad_parts, out_weight, attended, inv):
    rows = attended.shape[0]
    parts, step = grad_parts.shape[:2]
    return pl.pallas_call(
        out_kernel,
        out_shape=(
            jax.ShapeDtypeStruct((SIDE, parts // SIDE * step // 2, HD), F32),
            jax.ShapeDtypeStruct((SIDE, parts // SIDE * step // 2, HD), F32),
            jax.ShapeDtypeStruct((rows, HD), BF16),
            jax.ShapeDtypeStruct((8, rows), F32),
            jax.ShapeDtypeStruct((rows, HD), F32),
        ),
        in_specs=[pl.BlockSpec(memory_space=pltpu.VMEM)] * 4,
        out_specs=(pl.BlockSpec(memory_space=pltpu.VMEM),) * 5,
        compiler_params=pltpu.CompilerParams(vmem_limit_bytes=VMEM_LIMIT),
        name="out_grads",
    )(grad_parts, out_weight, attended, inv)


def root_back(grad_unit, values):
    factor = lax.rsqrt(jnp.mean(values * values, -1, keepdims=True) + EPS_ROOT)
    unit = values * factor
    return factor * (grad_unit - unit * jnp.mean(grad_unit * unit, -1, keepdims=True))


def back_kernel(
    slots_ref,
    proj_ref,
    query_ref,
    kv_ref,
    gatt_ref,
    stats_ref,
    inv_ref,
    delta_ref,
    out_ref,
    dq_ref,
    dk_ref,
    dv_ref,
):
    me = lax.axis_index("tile")
    mine = slots_ref[me]
    dq_ref[...] = jnp.zeros_like(dq_ref)
    dk_ref[...] = jnp.zeros_like(dk_ref)
    dv_ref[...] = jnp.zeros_like(dv_ref)
    my_inv = inv_ref[:, 0:1]
    my_delta = delta_ref[:, 0:1]

    @pl.loop(0, kv_ref.shape[0])
    def _(j):
        @pl.when(near(mine, slots_ref[j]))
        def _():
            key_j = kv_ref[j, :, :HD]
            scores = lax.dot_general(query_ref[me], key_j, NT, preferred_element_type=F32)
            probs = jnp.exp(scores * ATT_SCALE) * my_inv
            gprobs = lax.dot_general(
                gatt_ref[me], kv_ref[j, :, HD:], NT, preferred_element_type=F32
            )
            gscores = (probs * (gprobs - my_delta)).astype(BF16)
            dq_ref[...] += jnp.dot(gscores, key_j, preferred_element_type=F32)

            query_j = query_ref[j]
            gatt_j = gatt_ref[j]
            scores_t = lax.dot_general(
                kv_ref[me, :, :HD], query_j, NT, preferred_element_type=F32
            )
            probs_t = jnp.exp(scores_t * ATT_SCALE) * stats_ref[j, 0:1, :]
            dv_ref[...] += jnp.dot(probs_t.astype(BF16), gatt_j, preferred_element_type=F32)
            gprobs_t = lax.dot_general(
                kv_ref[me, :, HD:], gatt_j, NT, preferred_element_type=F32
            )
            gscores_t = (probs_t * (gprobs_t - stats_ref[j, 4:5, :])).astype(BF16)
            dk_ref[...] += jnp.dot(gscores_t, query_j, preferred_element_type=F32)

    out_ref[:, :HD] = root_back(dq_ref[...] * ATT_SCALE, proj_ref[:, :HD]).astype(BF16)
    out_ref[:, HD : 2 * HD] = root_back(
        dk_ref[...] * ATT_SCALE, proj_ref[:, HD : 2 * HD]
    ).astype(BF16)
    out_ref[:, 2 * HD :] = dv_ref[...].astype(BF16)


def attend_back(slots, projected, all_query, all_kv, all_gatt, all_stats, inv, delta):
    rows = projected.shape[0]
    return pl.pallas_call(
        back_kernel,
        out_shape=jax.ShapeDtypeStruct((rows, 3 * HD), BF16),
        in_specs=[pl.BlockSpec(memory_space=pltpu.SMEM)]
        + [pl.BlockSpec(memory_space=pltpu.VMEM)] * 7,
        out_specs=pl.BlockSpec(memory_space=pltpu.VMEM),
        scratch_shapes=[pltpu.VMEM((rows, HD), F32)] * 3,
        compiler_params=pltpu.CompilerParams(vmem_limit_bytes=VMEM_LIMIT),
        name="attend_back",
    )(slots, projected, all_query, all_kv, all_gatt, all_stats, inv, delta)


def terms_kernel(normed_ref, grad_ref, yparts_ref, zparts_ref, qkv_ref, ysum_ref, zsum_ref):
    step = qkv_ref.shape[1]
    for k in range(qkv_ref.shape[0]):
        total = None
        for j in range(normed_ref.shape[0]):
            term = lax.dot_general(
                normed_ref[j, :, k * step : (k + 1) * step],
                grad_ref[j],
                (((0,), (0,)), ((), ())),
                preferred_element_type=F32,
            )
            total = term if total is None else total + term
        qkv_ref[k] = total
    for parts_ref, sum_ref in ((yparts_ref, ysum_ref), (zparts_ref, zsum_ref)):
        half = sum_ref.shape[1]
        for k in range(sum_ref.shape[0]):
            rows = slice(k * half, (k + 1) * half)
            sum_ref[k] = parts_ref[0, rows] + (parts_ref[1, rows] + parts_ref[2, rows])


def grad_terms(normed_parts, qkv_parts, yparts, zparts):
    step = normed_parts.shape[2] // SIDE
    half = yparts.shape[1] // SIDE
    return pl.pallas_call(
        terms_kernel,
        out_shape=(
            jax.ShapeDtypeStruct((SIDE, step, 3 * HD), F32),
            jax.ShapeDtypeStruct((SIDE, half, HD), F32),
            jax.ShapeDtypeStruct((SIDE, half, HD), F32),
        ),
        in_specs=[pl.BlockSpec(memory_space=pltpu.VMEM)] * 4,
        out_specs=(pl.BlockSpec(memory_space=pltpu.VMEM),) * 3,
        compiler_params=pltpu.CompilerParams(vmem_limit_bytes=VMEM_LIMIT),
        name="grad_terms",
    )(normed_parts, qkv_parts, yparts, zparts)


def sums_kernel(qkv_ref, first_ref, second_ref, qkv_out_ref, out_out_ref):
    qkv_out_ref[...] = qkv_ref[0] + (qkv_ref[1] + qkv_ref[2])
    first = first_ref[0] + (first_ref[1] + first_ref[2])
    second = second_ref[0] + (second_ref[1] + second_ref[2])
    half = first.shape[0]
    out_out_ref[:half, :] = first
    out_out_ref[half:, :] = second


def final_sums(qkv_pieces, first, second):
    step = qkv_pieces.shape[1]
    return pl.pallas_call(
        sums_kernel,
        out_shape=(
            jax.ShapeDtypeStruct((step, 3 * HD), F32),
            jax.ShapeDtypeStruct((step, HD), F32),
        ),
        in_specs=[pl.BlockSpec(memory_space=pltpu.VMEM)] * 3,
        out_specs=(pl.BlockSpec(memory_space=pltpu.VMEM),) * 2,
        compiler_params=pltpu.CompilerParams(vmem_limit_bytes=VMEM_LIMIT),
        name="final_sums",
    )(qkv_pieces, first, second)


def modulated_norm(tokens, mod_shift, mod_scale):
    values_in = tokens.astype(F32)
    center = values_in - jnp.mean(values_in, -1, keepdims=True)
    spread = jnp.mean(center * center, -1, keepdims=True)
    return (center * lax.rsqrt(spread + EPS_NORM) * (1.0 + mod_scale) + mod_shift).astype(BF16)


def root_norm(values):
    return values * lax.rsqrt(jnp.mean(values * values, -1, keepdims=True) + EPS_ROOT)


def per_device(tokens, mod_shift, mod_scale, mod_gate, qkv_weight, out_weight, teacher, slot_tiles):
    width = out_weight.shape[1]
    step = width // 16
    head = lax.axis_index("head")
    normed = modulated_norm(tokens, mod_shift, mod_scale)
    projected = jnp.dot(normed, qkv_weight, preferred_element_type=F32)
    query_b = root_norm(projected[:, :HD]).astype(BF16)
    key_b = root_norm(projected[:, HD : 2 * HD]).astype(BF16)
    kv = jnp.concatenate([key_b, projected[:, 2 * HD :].astype(BF16)], 1)
    weight_t = out_weight.T.reshape(16, step, HD)
    teacher_part = lax.dynamic_slice_in_dim(teacher, head * step, step, 1).T
    gate_part = lax.dynamic_slice_in_dim(mod_gate, head * step, step, 0)[:, None]

    all_kv, weight_parts = exchange("share_kv", 1, ("tag", kv), ("ha2a", weight_t))
    attended, inv = attend(slot_tiles, query_b, all_kv)
    att_parts, all_query = exchange("share_att", 2, ("hag", attended), ("tag", query_b))
    grad_part = branch_grad(weight_parts, att_parts, teacher_part, gate_part)
    grad_parts, normed_parts = exchange("share_grad", 3, ("hag", grad_part), ("ycols", normed))
    yterm, zterm, gatt, stats, delta = out_grads(grad_parts, out_weight, attended, inv)
    all_gatt, all_stats = exchange("share_gatt", 4, ("tag", gatt), ("tag", stats))
    grad_qkv = attend_back(
        slot_tiles, projected, all_query, all_kv, all_gatt, all_stats, inv, delta
    )
    qkv_parts, yparts, zparts = exchange(
        "share_qkv", 5, ("yag", grad_qkv), ("yrs", yterm), ("zrs", zterm)
    )
    qkv_term, ysum, zsum = grad_terms(normed_parts, qkv_parts, yparts, zparts)
    qkv_grad, out_grad = final_sums(
        *exchange("share_sums", 6, ("zrs", qkv_term), ("zrs", ysum), ("yrs", zsum))
    )
    return qkv_grad, out_grad.T


def solution(mesh):
    return jax.shard_map(
        per_device,
        mesh=mesh,
        in_specs=(
            P("tile", None),
            P(),
            P(),
            P(),
            P(None, "head"),
            P("head", None),
            P("tile", None),
            P(),
        ),
        out_specs=(P("tile", "head"), P("head", "tile")),
        check_vma=False,
    )
```

```python
import functools
import math

import jax
import jax.numpy as jnp
from jax import lax
from jax.experimental import pallas as pl
from jax.experimental.pallas import tpu as pltpu
from jax.sharding import PartitionSpec as P

HD = 128
TOK_TILE = 384
TH = 4
TW = 4
SIDE = 4
EPS_NORM = 1e-05
EPS_ROOT = 1e-06
LOSS_WEIGHT = 32.0
ATT_SCALE = 1.0 / math.sqrt(HD)
BF16 = jnp.bfloat16
F32 = jnp.float32
MESH = pl.DeviceIdType.MESH
NT = (((1,), (1,)), ((), ()))
VMEM_LIMIT = 24 * 1024 * 1024
COMM_LIMIT = 8 * 1024 * 1024


class Places:

    def __init__(self):
        self.t = lax.axis_index("tile")
        self.h = lax.axis_index("head")
        self.a = self.t // SIDE
        self.b = self.t % SIDE
        self.x = self.h // 4
        self.lo = self.h % 4

    def tile(self, j, k):
        return lax.rem(self.a + j, SIDE) * SIDE + lax.rem(self.b + k, SIDE)

    def head(self, j, flip):
        lo = self.lo
        if flip & 1:
            lo = lo + 1 - 2 * lax.rem(lo, 2)
        if flip & 2:
            lo = lax.rem(lo + 2, 4)
        return lax.rem(self.x + j, 4) * 4 + lo


TASK_SEMS = {"tag": 30, "hag": 22, "ha2a": 16, "ycols": 8, "yag": 25, "yrs": 6, "zrs": 6}


def task_peers(kind):
    if kind == "tag":
        return {("t", 0, 1), ("t", 0, 3), ("t", 1, 0), ("t", 3, 0)}
    if kind == "hag":
        return {("h", j, 0) for j in (1, 3)} | {("h", 0, 2), ("h", 0, 1)}
    if kind == "ha2a":
        return {("h", j, f) for j in range(4) for f in range(4)} - {("h", 0, 0)}
    if kind == "zrs":
        return {("t", 0, k) for k in (1, 3)}
    if kind in ("yag", "yrs"):
        return {("t", j, 0) for j in (1, 3)}
    if kind == "ycols":
        return {("t", j, 0) for j in (1, 2, 3)} | {("h", 0, 1)}
    raise ValueError(kind)


def out_slots(kind):
    if kind in ("yrs", "zrs"):
        return 3
    return 16 if kind in ("tag", "hag", "ha2a") else 4


def comm_kernel(kinds, *refs):
    n = len(kinds)
    ins, outs = refs[:n], refs[n : 2 * n]
    sems = refs[2 * n : 5 * n]
    holds = list(refs[5 * n :])
    at = Places()

    def device(peer):
        axis, j, k = peer
        if axis == "t":
            return (at.tile(j, k), at.h)
        return (at.t, at.head(j, k))

    peers = sorted(set().union(*[task_peers(kind) for kind in kinds]))
    barrier = pltpu.get_barrier_semaphore()
    for peer in peers:
        pl.semaphore_signal(barrier, inc=1, device_id=device(peer), device_id_type=MESH)
    pl.semaphore_wait(barrier, len(peers))

    started = []
    locals_ = []

    def send(i, src, dst, index, peer):
        copy = pltpu.make_async_remote_copy(
            src_ref=src,
            dst_ref=dst,
            send_sem=sems[3 * i].at[index],
            recv_sem=sems[3 * i + 1].at[index],
            device_id=device(peer),
            device_id_type=MESH,
        )
        copy.start()
        started.append(copy)

    def arrive(i, dst, index, peer):
        pltpu.make_async_remote_copy(
            src_ref=dst,
            dst_ref=dst,
            send_sem=sems[3 * i].at[index],
            recv_sem=sems[3 * i + 1].at[index],
            device_id=device(peer),
            device_id_type=MESH,
        ).wait_recv()

    def keep(i, src, slot):
        copy = pltpu.make_async_copy(src, outs[i].at[slot], sems[3 * i + 2].at[0])
        copy.start()
        locals_.append(copy)

    steps = []
    for i, kind in enumerate(kinds):
        src = ins[i]
        out = outs[i]

        def half(slot, part, out=out):
            rows = out.shape[1] // 2
            if rows < 8:
                return out.at[slot, :, pl.ds(*((0, 256), (256, out.shape[2] - 256))[part])]
            return out.at[slot, pl.ds(part * rows, rows)]

        if kind in ("tag", "hag", "yag"):
            axis = "h" if kind == "hag" else "t"

            def slot_of(j, k, kind=kind):
                if kind == "hag":
                    return at.head(j, 2 * k)
                if kind == "tag":
                    return at.tile(j, k)
                return lax.rem(at.a + j, SIDE)

            def own(part, src=src):
                rows = src.shape[0] // 2
                if rows < 8:
                    return src.at[:, pl.ds(*((0, 256), (256, src.shape[1] - 256))[part])]
                return src.at[pl.ds(part * rows, rows)]

            rest = 18 if kind == "hag" else 20
            gap = 2 if kind == "hag" else 4

            def spread(
                i, k, block=None, axis=axis, slot_of=slot_of, half=half, rest=rest, gap=gap
            ):
                slot = slot_of(0, 4 - k if axis == "t" and k else k)
                for late in (0, 1):
                    for j, first in ((1, 0), (3, 1)):
                        part = first ^ late
                        piece = half(slot, part) if block is None else block(part)
                        index = rest + gap * first + k if late else 4 * j + k
                        send(i, piece, half(slot, part), index, (axis, j, 0))

            def relay(i, k, axis=axis, slot_of=slot_of, half=half):
                back = 4 - k if axis == "t" and k else k
                for j, part in ((1, 0), (3, 1)):
                    piece = half(slot_of(4 - j, back), part)
                    arrive(i, piece, 4 * j + k, (axis, j, 0))
                    send(i, piece, piece, (8 + k, k)[part], (axis, j, 0))

            def settle(i, k, axis=axis, slot_of=slot_of, half=half, out=out, rest=rest, gap=gap, kind=kind):
                back = 4 - k if axis == "t" and k else k
                for j, part in ((1, 0), (3, 1)):
                    slot = slot_of(4 - j, back)
                    arrive(i, half(slot, 1 - part), rest + gap * part + k, (axis, j, 0))
                    if kind == "hag":
                        send(i, out.at[slot], out.at[slot], 4 * j + 2 + k, ("h", 0, 1))

            def far(i, k, axis=axis, slot_of=slot_of, half=half, out=out, kind=kind):
                back = 4 - k if axis == "t" and k else k
                slot = slot_of(2, back)
                arrive(i, half(slot, 0), 8 + k, (axis, 1, 0))
                arrive(i, half(slot, 1), k, (axis, 3, 0))
                if kind == "hag":
                    send(i, out.at[slot], out.at[slot], 10 + k, ("h", 0, 1))

            if kind == "tag":
                for late in (0, 1):
                    for k, first in ((1, 0), (3, 1)):
                        part = first ^ late
                        index = 28 + first if late else 16 + k
                        send(i, own(part), half(at.t, part), index, ("t", 0, k))
                spread(i, 0, own)
                keep(i, src, at.t)

                def onward(i=i, spread=spread, half=half):
                    for k, part in ((1, 0), (3, 1)):
                        piece = half(at.tile(0, 4 - k), part)
                        arrive(i, piece, 16 + k, ("t", 0, k))
                        send(i, piece, piece, (16, 18)[part], ("t", 0, k))
                    for k, part in ((1, 0), (3, 1)):
                        arrive(i, half(at.tile(0, 4 - k), 1 - part), 28 + part, ("t", 0, k))
                        spread(i, k)

                def last(i=i, out=out, spread=spread, half=half):
                    slot = at.tile(0, 2)
                    arrive(i, half(slot, 0), 16, ("t", 0, 1))
                    arrive(i, half(slot, 1), 18, ("t", 0, 3))
                    spread(i, 2)

                steps.append((2, functools.partial(relay, i, 0)))
                steps.append((3, onward))
                steps.append((4.5, functools.partial(relay, i, 1)))
                steps.append((5, last))
                steps.append((5.5, functools.partial(relay, i, 3)))
                steps.append((7, functools.partial(relay, i, 2)))
                for k in (0, 1, 3, 2):
                    steps.append((1000, functools.partial(settle, i, k)))
                    steps.append((1000, functools.partial(far, i, k)))
            elif kind == "hag":
                send(i, src, out.at[at.h], 16, ("h", 0, 2))
                spread(i, 0, own)
                send(i, src, out.at[at.h], 2, ("h", 0, 1))
                keep(i, src, at.h)

                def onward(i=i, out=out, spread=spread):
                    slot = at.head(0, 2)
                    arrive(i, out.at[slot], 16, ("h", 0, 2))
                    spread(i, 1)
                    send(i, out.at[slot], out.at[slot], 3, ("h", 0, 1))

                def finish(i=i, out=out):
                    for k in (0, 1):
                        for j in range(4):
                            slot = at.head(4 - j, 2 * k + 1)
                            arrive(i, out.at[slot], 4 * j + 2 + k, ("h", 0, 1))

                steps.append((1, onward))
                steps.append((1.5, functools.partial(relay, i, 0)))
                steps.append((1.6, functools.partial(settle, i, 0)))
                steps.append((3.2, functools.partial(relay, i, 1)))
                steps.append((4.5, functools.partial(settle, i, 1)))
                steps.append((4, functools.partial(far, i, 0)))
                steps.append((5.2, functools.partial(far, i, 1)))
                steps.append((1001, finish))
            else:
                spread(i, 0, own)
                keep(i, src, at.a)
                steps.append((1, functools.partial(relay, i, 0)))
                steps.append((1000, functools.partial(settle, i, 0)))
                steps.append((1000, functools.partial(far, i, 0)))
        elif kind == "ha2a":
            def give(i=i, src=src, out=out, flips=()):
                for f in flips:
                    for j in range(4):
                        if f or j:
                            send(i, src.at[at.head(j, f)], out.at[at.h], 4 * f + j, ("h", j, f))

            give(flips=(1, 0))
            keep(i, src.at[at.h], at.h)
            steps.append((5, functools.partial(give, flips=(3, 2))))

            def finish(i=i, out=out):
                for f in range(4):
                    for j in range(4):
                        if f or j:
                            arrive(i, out.at[at.head(4 - j, f)], 4 * f + j, ("h", j, f))

            steps.append((1000, finish))
        elif kind == "ycols":
            width = src.shape[1] // SIDE
            rows = src.shape[0] // 2
            mine = pl.ds(pl.multiple_of(lax.rem(at.h, 2) * rows, rows), rows)
            other = pl.ds(pl.multiple_of((1 - lax.rem(at.h, 2)) * rows, rows), rows)

            def columns(j, width=width):
                return pl.ds(pl.multiple_of(lax.rem(at.a + j, SIDE) * width, 128), width)

            for j in (2, 1, 3):
                send(i, src.at[mine, columns(j)], out.at[at.a, mine], j, ("t", j, 0))
            keep(i, src.at[:, columns(0)], at.a)

            def share(i=i, out=out, mine=mine):
                for j in (1, 3, 2):
                    block = out.at[lax.rem(at.a + 4 - j, SIDE), mine]
                    arrive(i, block, j, ("t", j, 0))
                    send(i, block, block, 4 + j, ("h", 0, 1))

            def finish(i=i, out=out, other=other):
                for j in (1, 3, 2):
                    block = out.at[lax.rem(at.a + 4 - j, SIDE), other]
                    arrive(i, block, 4 + j, ("h", 0, 1))

            steps.append((999, share))
            steps.append((1002, finish))
        else:
            along_z = kind == "zrs"
            held, summed = holds.pop(0), holds.pop(0)

            def spot(j, along_z=along_z):
                return lax.rem((at.b if along_z else at.a) + j, SIDE)

            def peer_of(j, along_z=along_z):
                return ("t", 0, j) if along_z else ("t", j, 0)

            rows = src.shape[1] // 2
            parts = (pl.ds(0, rows), pl.ds(rows, rows))
            for part, j in ((0, 1), (1, 3)):
                send(i, src.at[spot(2), parts[part]], held.at[part], part, peer_of(j))
            for part, j in ((0, 1), (1, 3)):
                rest = parts[1 - part]
                send(i, src.at[spot(j), rest], out.at[1 + part, rest], 2 + part, peer_of(j))
            keep(i, src.at[spot(0)], 0)

            def add(
                i=i, src=src, out=out, held=held, summed=summed, spot=spot, peer_of=peer_of, parts=parts
            ):
                for part, j in ((0, 1), (1, 3)):
                    arrive(i, held.at[part], part, peer_of(j))
                    summed[part] = src[spot(j), parts[part], :] + held[part]
                for part, j in ((0, 1), (1, 3)):
                    send(i, summed.at[part], out.at[1 + part, parts[part]], 4 + part, peer_of(j))

            def finish(i=i, out=out, peer_of=peer_of, parts=parts):
                for part, j in ((0, 1), (1, 3)):
                    arrive(i, out.at[1 + part, parts[1 - part]], 2 + part, peer_of(j))
                    arrive(i, out.at[1 + part, parts[part]], 4 + part, peer_of(j))

            steps.append((2, add))
            steps.append((1000, finish))

    for _, step in sorted(steps, key=lambda step: step[0]):
        step()
    for copy in started:
        copy.wait_send()
    for copy in locals_:
        copy.wait()


def exchange(name, cid, *tasks):
    kinds = tuple(kind for kind, _ in tasks)
    arrays = [array for _, array in tasks]
    shapes = []
    for kind, array in tasks:
        if kind in ("tag", "hag", "yag"):
            piece = array.shape
        elif kind == "ycols":
            piece = (array.shape[0], array.shape[1] // SIDE)
        else:
            piece = array.shape[1:]
        shapes.append(jax.ShapeDtypeStruct((out_slots(kind),) + piece, array.dtype))
    scratch = []
    for kind in kinds:
        scratch += [
            pltpu.SemaphoreType.DMA((TASK_SEMS[kind],)),
            pltpu.SemaphoreType.DMA((TASK_SEMS[kind],)),
            pltpu.SemaphoreType.DMA((1,)),
        ]
    for kind, array in tasks:
        if kind in ("yrs", "zrs"):
            piece = (2, array.shape[1] // 2) + array.shape[2:]
            scratch += [pltpu.VMEM(piece, array.dtype)] * 2
    return pl.pallas_call(
        functools.partial(comm_kernel, kinds),
        out_shape=shapes,
        in_specs=[pl.BlockSpec(memory_space=pltpu.VMEM)] * len(arrays),
        out_specs=[pl.BlockSpec(memory_space=pltpu.VMEM)] * len(arrays),
        scratch_shapes=scratch,
        compiler_params=pltpu.CompilerParams(
            collective_id=cid, has_side_effects=True, vmem_limit_bytes=COMM_LIMIT
        ),
        name=name,
    )(*arrays)


def near(first, second):
    def coords(ids):
        return ids // (TH * TW), ids // TW % TH, ids % TW

    close = True
    for one, two in zip(coords(first), coords(second)):
        close = close & (jnp.abs(one - two) <= 1)
    return close


def attend_kernel(slots_ref, query_ref, kv_ref, att_ref, inv_ref, exp_ref, total_ref, acc_ref):
    mine = slots_ref[lax.axis_index("tile")]
    total_ref[...] = jnp.zeros_like(total_ref)
    acc_ref[...] = jnp.zeros_like(acc_ref)
    count = kv_ref.shape[0]

    @pl.loop(0, count)
    def _(j):
        @pl.when(near(mine, slots_ref[j]))
        def _():
            scores = lax.dot_general(
                query_ref[...], kv_ref[j, :, :HD], NT, preferred_element_type=F32
            )
            grown = jnp.exp(scores * ATT_SCALE)
            exp_ref[j] = grown
            total_ref[...] += jnp.sum(grown, -1, keepdims=True)

    inv = 1.0 / total_ref[...]
    inv_ref[...] = jnp.broadcast_to(inv, inv_ref.shape)

    @pl.loop(0, count)
    def _(j):
        @pl.when(near(mine, slots_ref[j]))
        def _():
            probs = (exp_ref[j] * inv).astype(BF16)
            acc_ref[...] += jnp.dot(probs, kv_ref[j, :, HD:], preferred_element_type=F32)

    att_ref[...] = acc_ref[...].astype(BF16)


def attend(slots, query_b, all_kv):
    rows = query_b.shape[0]
    return pl.pallas_call(
        attend_kernel,
        out_shape=(
            jax.ShapeDtypeStruct((rows, HD), BF16),
            jax.ShapeDtypeStruct((rows, HD), F32),
        ),
        in_specs=[
            pl.BlockSpec(memory_space=pltpu.SMEM),
            pl.BlockSpec(memory_space=pltpu.VMEM),
            pl.BlockSpec(memory_space=pltpu.VMEM),
        ],
        out_specs=(
            pl.BlockSpec(memory_space=pltpu.VMEM),
            pl.BlockSpec(memory_space=pltpu.VMEM),
        ),
        scratch_shapes=[
            pltpu.VMEM((all_kv.shape[0], rows, rows), F32),
            pltpu.VMEM((rows, 1), F32),
            pltpu.VMEM((rows, HD), F32),
        ],
        compiler_params=pltpu.CompilerParams(vmem_limit_bytes=VMEM_LIMIT),
        name="attend",
    )(slots, query_b, all_kv)


def branch_kernel(weight_ref, att_ref, teacher_ref, gate_ref, grad_ref):
    total = None
    for h in range(att_ref.shape[0]):
        term = lax.dot_general(weight_ref[h], att_ref[h], NT, preferred_element_type=F32)
        total = term if total is None else total + term
    gate = gate_ref[...]
    residual = LOSS_WEIGHT * (gate * total - teacher_ref[...].astype(F32))
    grad_ref[...] = (gate * residual).astype(BF16)


def branch_grad(weight_parts, att_parts, teacher_part, gate_part):
    return pl.pallas_call(
        branch_kernel,
        out_shape=jax.ShapeDtypeStruct(teacher_part.shape, BF16),
        in_specs=[pl.BlockSpec(memory_space=pltpu.VMEM)] * 4,
        out_specs=pl.BlockSpec(memory_space=pltpu.VMEM),
        compiler_params=pltpu.CompilerParams(vmem_limit_bytes=VMEM_LIMIT),
        name="branch_grad",
    )(weight_parts, att_parts, teacher_part, gate_part)


def out_kernel(
    grad_ref,
    weight_ref,
    att_ref,
    inv_ref,
    yterm_ref,
    zterm_ref,
    gatt_ref,
    stats_ref,
    delta_ref,
):
    rows = att_ref.shape[0]
    step = grad_ref.shape[1]
    half = step // 2
    grad_t = jnp.zeros((HD, rows), F32)
    for h in range(grad_ref.shape[0]):
        block = grad_ref[h]
        grad_t += jnp.dot(
            weight_ref[:, h * step : (h + 1) * step], block, preferred_element_type=F32
        )
        term = jnp.dot(block, att_ref[...], preferred_element_type=F32)
        low = h % SIDE * half
        yterm_ref[h // SIDE, low : low + half, :] = term[:half]
        low = h // SIDE * half
        zterm_ref[h % SIDE, low : low + half, :] = term[half:]
    gatt = grad_t.T.astype(BF16)
    gatt_ref[...] = gatt
    delta = jnp.sum(gatt.astype(F32) * att_ref[...].astype(F32), -1, keepdims=True)
    delta_all = jnp.broadcast_to(delta, (rows, HD))
    delta_ref[...] = delta_all
    stats_ref[0:4, :] = inv_ref[...].T[0:4]
    stats_ref[4:8, :] = delta_all.T[0:4]


def out_grads(grad_parts, out_weight, attended, inv):
    rows = attended.shape[0]
    parts, step = grad_parts.shape[:2]
    return pl.pallas_call(
        out_kernel,
        out_shape=(
            jax.ShapeDtypeStruct((SIDE, parts // SIDE * step // 2, HD), F32),
            jax.ShapeDtypeStruct((SIDE, parts // SIDE * step // 2, HD), F32),
            jax.ShapeDtypeStruct((rows, HD), BF16),
            jax.ShapeDtypeStruct((8, rows), F32),
            jax.ShapeDtypeStruct((rows, HD), F32),
        ),
        in_specs=[pl.BlockSpec(memory_space=pltpu.VMEM)] * 4,
        out_specs=(pl.BlockSpec(memory_space=pltpu.VMEM),) * 5,
        compiler_params=pltpu.CompilerParams(vmem_limit_bytes=VMEM_LIMIT),
        name="out_grads",
    )(grad_parts, out_weight, attended, inv)


def root_back(grad_unit, values):
    factor = lax.rsqrt(jnp.mean(values * values, -1, keepdims=True) + EPS_ROOT)
    unit = values * factor
    return factor * (grad_unit - unit * jnp.mean(grad_unit * unit, -1, keepdims=True))


def back_kernel(
    slots_ref,
    proj_ref,
    query_ref,
    kv_ref,
    gatt_ref,
    stats_ref,
    inv_ref,
    delta_ref,
    out_ref,
    dq_ref,
    dk_ref,
    dv_ref,
):
    me = lax.axis_index("tile")
    mine = slots_ref[me]
    dq_ref[...] = jnp.zeros_like(dq_ref)
    dk_ref[...] = jnp.zeros_like(dk_ref)
    dv_ref[...] = jnp.zeros_like(dv_ref)
    my_inv = inv_ref[:, 0:1]
    my_delta = delta_ref[:, 0:1]

    @pl.loop(0, kv_ref.shape[0])
    def _(j):
        @pl.when(near(mine, slots_ref[j]))
        def _():
            key_j = kv_ref[j, :, :HD]
            scores = lax.dot_general(query_ref[me], key_j, NT, preferred_element_type=F32)
            probs = jnp.exp(scores * ATT_SCALE) * my_inv
            gprobs = lax.dot_general(
                gatt_ref[me], kv_ref[j, :, HD:], NT, preferred_element_type=F32
            )
            gscores = (probs * (gprobs - my_delta)).astype(BF16)
            dq_ref[...] += jnp.dot(gscores, key_j, preferred_element_type=F32)

            query_j = query_ref[j]
            gatt_j = gatt_ref[j]
            scores_t = lax.dot_general(
                kv_ref[me, :, :HD], query_j, NT, preferred_element_type=F32
            )
            probs_t = jnp.exp(scores_t * ATT_SCALE) * stats_ref[j, 0:1, :]
            dv_ref[...] += jnp.dot(probs_t.astype(BF16), gatt_j, preferred_element_type=F32)
            gprobs_t = lax.dot_general(
                kv_ref[me, :, HD:], gatt_j, NT, preferred_element_type=F32
            )
            gscores_t = (probs_t * (gprobs_t - stats_ref[j, 4:5, :])).astype(BF16)
            dk_ref[...] += jnp.dot(gscores_t, query_j, preferred_element_type=F32)

    out_ref[:, :HD] = root_back(dq_ref[...] * ATT_SCALE, proj_ref[:, :HD]).astype(BF16)
    out_ref[:, HD : 2 * HD] = root_back(
        dk_ref[...] * ATT_SCALE, proj_ref[:, HD : 2 * HD]
    ).astype(BF16)
    out_ref[:, 2 * HD :] = dv_ref[...].astype(BF16)


def attend_back(slots, projected, all_query, all_kv, all_gatt, all_stats, inv, delta):
    rows = projected.shape[0]
    return pl.pallas_call(
        back_kernel,
        out_shape=jax.ShapeDtypeStruct((rows, 3 * HD), BF16),
        in_specs=[pl.BlockSpec(memory_space=pltpu.SMEM)]
        + [pl.BlockSpec(memory_space=pltpu.VMEM)] * 7,
        out_specs=pl.BlockSpec(memory_space=pltpu.VMEM),
        scratch_shapes=[pltpu.VMEM((rows, HD), F32)] * 3,
        compiler_params=pltpu.CompilerParams(vmem_limit_bytes=VMEM_LIMIT),
        name="attend_back",
    )(slots, projected, all_query, all_kv, all_gatt, all_stats, inv, delta)


def terms_kernel(normed_ref, grad_ref, yparts_ref, zparts_ref, qkv_ref, ysum_ref, zsum_ref):
    step = qkv_ref.shape[1]
    for k in range(qkv_ref.shape[0]):
        total = None
        for j in range(normed_ref.shape[0]):
            term = lax.dot_general(
                normed_ref[j, :, k * step : (k + 1) * step],
                grad_ref[j],
                (((0,), (0,)), ((), ())),
                preferred_element_type=F32,
            )
            total = term if total is None else total + term
        qkv_ref[k] = total
    for parts_ref, sum_ref in ((yparts_ref, ysum_ref), (zparts_ref, zsum_ref)):
        half = sum_ref.shape[1]
        for k in range(sum_ref.shape[0]):
            rows = slice(k * half, (k + 1) * half)
            sum_ref[k] = parts_ref[0, rows] + (parts_ref[1, rows] + parts_ref[2, rows])


def grad_terms(normed_parts, qkv_parts, yparts, zparts):
    step = normed_parts.shape[2] // SIDE
    half = yparts.shape[1] // SIDE
    return pl.pallas_call(
        terms_kernel,
        out_shape=(
            jax.ShapeDtypeStruct((SIDE, step, 3 * HD), F32),
            jax.ShapeDtypeStruct((SIDE, half, HD), F32),
            jax.ShapeDtypeStruct((SIDE, half, HD), F32),
        ),
        in_specs=[pl.BlockSpec(memory_space=pltpu.VMEM)] * 4,
        out_specs=(pl.BlockSpec(memory_space=pltpu.VMEM),) * 3,
        compiler_params=pltpu.CompilerParams(vmem_limit_bytes=VMEM_LIMIT),
        name="grad_terms",
    )(normed_parts, qkv_parts, yparts, zparts)


def sums_kernel(qkv_ref, first_ref, second_ref, qkv_out_ref, out_out_ref):
    qkv_out_ref[...] = qkv_ref[0] + (qkv_ref[1] + qkv_ref[2])
    first = first_ref[0] + (first_ref[1] + first_ref[2])
    second = second_ref[0] + (second_ref[1] + second_ref[2])
    half = first.shape[0]
    out_out_ref[:half, :] = first
    out_out_ref[half:, :] = second


def final_sums(qkv_pieces, first, second):
    step = qkv_pieces.shape[1]
    return pl.pallas_call(
        sums_kernel,
        out_shape=(
            jax.ShapeDtypeStruct((step, 3 * HD), F32),
            jax.ShapeDtypeStruct((step, HD), F32),
        ),
        in_specs=[pl.BlockSpec(memory_space=pltpu.VMEM)] * 3,
        out_specs=(pl.BlockSpec(memory_space=pltpu.VMEM),) * 2,
        compiler_params=pltpu.CompilerParams(vmem_limit_bytes=VMEM_LIMIT),
        name="final_sums",
    )(qkv_pieces, first, second)


def modulated_norm(tokens, mod_shift, mod_scale):
    values_in = tokens.astype(F32)
    center = values_in - jnp.mean(values_in, -1, keepdims=True)
    spread = jnp.mean(center * center, -1, keepdims=True)
    return (center * lax.rsqrt(spread + EPS_NORM) * (1.0 + mod_scale) + mod_shift).astype(BF16)


def root_norm(values):
    return values * lax.rsqrt(jnp.mean(values * values, -1, keepdims=True) + EPS_ROOT)


def per_device(tokens, mod_shift, mod_scale, mod_gate, qkv_weight, out_weight, teacher, slot_tiles):
    width = out_weight.shape[1]
    step = width // 16
    head = lax.axis_index("head")
    normed = modulated_norm(tokens, mod_shift, mod_scale)
    projected = jnp.dot(normed, qkv_weight, preferred_element_type=F32)
    query_b = root_norm(projected[:, :HD]).astype(BF16)
    key_b = root_norm(projected[:, HD : 2 * HD]).astype(BF16)
    kv = jnp.concatenate([key_b, projected[:, 2 * HD :].astype(BF16)], 1)
    weight_t = out_weight.T.reshape(16, step, HD)
    teacher_part = lax.dynamic_slice_in_dim(teacher, head * step, step, 1).T
    gate_part = lax.dynamic_slice_in_dim(mod_gate, head * step, step, 0)[:, None]

    all_kv, weight_parts = exchange("share_kv", 1, ("tag", kv), ("ha2a", weight_t))
    attended, inv = attend(slot_tiles, query_b, all_kv)
    att_parts, all_query = exchange("share_att", 2, ("hag", attended), ("tag", query_b))
    grad_part = branch_grad(weight_parts, att_parts, teacher_part, gate_part)
    grad_parts, normed_parts = exchange("share_grad", 3, ("hag", grad_part), ("ycols", normed))
    yterm, zterm, gatt, stats, delta = out_grads(grad_parts, out_weight, attended, inv)
    all_gatt, all_stats = exchange("share_gatt", 4, ("tag", gatt), ("tag", stats))
    grad_qkv = attend_back(
        slot_tiles, projected, all_query, all_kv, all_gatt, all_stats, inv, delta
    )
    qkv_parts, yparts, zparts = exchange(
        "share_qkv", 5, ("yag", grad_qkv), ("yrs", yterm), ("zrs", zterm)
    )
    qkv_term, ysum, zsum = grad_terms(normed_parts, qkv_parts, yparts, zparts)
    qkv_grad, out_grad = final_sums(
        *exchange("share_sums", 6, ("zrs", qkv_term), ("zrs", ysum), ("yrs", zsum))
    )
    return qkv_grad, out_grad.T


def solution(mesh):
    return jax.shard_map(
        per_device,
        mesh=mesh,
        in_specs=(
            P("tile", None),
            P(),
            P(),
            P(),
            P(None, "head"),
            P("head", None),
            P("tile", None),
            P(),
        ),
        out_specs=(P("tile", "head"), P("head", "tile")),
        check_vma=False,
    )
```

```python
import functools
import math

import jax
import jax.numpy as jnp
from jax import lax
from jax.experimental import pallas as pl
from jax.experimental.pallas import tpu as pltpu
from jax.sharding import PartitionSpec as P

HD = 128
TOK_TILE = 384
TH = 4
TW = 4
SIDE = 4
EPS_NORM = 1e-05
EPS_ROOT = 1e-06
LOSS_WEIGHT = 32.0
ATT_SCALE = 1.0 / math.sqrt(HD)
BF16 = jnp.bfloat16
F32 = jnp.float32
MESH = pl.DeviceIdType.MESH
NT = (((1,), (1,)), ((), ()))
VMEM_LIMIT = 24 * 1024 * 1024
COMM_LIMIT = 8 * 1024 * 1024


class Places:

    def __init__(self):
        self.t = lax.axis_index("tile")
        self.h = lax.axis_index("head")
        self.a = self.t // SIDE
        self.b = self.t % SIDE
        self.x = self.h // 4
        self.lo = self.h % 4

    def tile(self, j, k):
        return lax.rem(self.a + j, SIDE) * SIDE + lax.rem(self.b + k, SIDE)

    def head(self, j, flip):
        lo = self.lo
        if flip & 1:
            lo = lo + 1 - 2 * lax.rem(lo, 2)
        if flip & 2:
            lo = lax.rem(lo + 2, 4)
        return lax.rem(self.x + j, 4) * 4 + lo


TASK_SEMS = {"tag": 30, "hag": 22, "ha2a": 16, "ycols": 8, "yag": 25, "yrs": 6, "zrs": 6}


def task_peers(kind):
    if kind == "tag":
        return {("t", 0, 1), ("t", 0, 3), ("t", 1, 0), ("t", 3, 0)}
    if kind == "hag":
        return {("h", j, 0) for j in (1, 3)} | {("h", 0, 2), ("h", 0, 1)}
    if kind == "ha2a":
        return {("h", j, f) for j in range(4) for f in range(4)} - {("h", 0, 0)}
    if kind == "zrs":
        return {("t", 0, k) for k in (1, 3)}
    if kind in ("yag", "yrs"):
        return {("t", j, 0) for j in (1, 3)}
    if kind == "ycols":
        return {("t", j, 0) for j in (1, 2, 3)} | {("h", 0, 1)}
    raise ValueError(kind)


def out_slots(kind):
    if kind in ("yrs", "zrs"):
        return 3
    return 16 if kind in ("tag", "hag", "ha2a") else 4


def comm_kernel(kinds, *refs):
    n = len(kinds)
    ins, outs = refs[:n], refs[n : 2 * n]
    sems = refs[2 * n : 5 * n]
    holds = list(refs[5 * n :])
    at = Places()

    def device(peer):
        axis, j, k = peer
        if axis == "t":
            return (at.tile(j, k), at.h)
        return (at.t, at.head(j, k))

    peers = sorted(set().union(*[task_peers(kind) for kind in kinds]))
    barrier = pltpu.get_barrier_semaphore()
    for peer in peers:
        pl.semaphore_signal(barrier, inc=1, device_id=device(peer), device_id_type=MESH)
    pl.semaphore_wait(barrier, len(peers))

    started = []
    locals_ = []

    def send(i, src, dst, index, peer):
        copy = pltpu.make_async_remote_copy(
            src_ref=src,
            dst_ref=dst,
            send_sem=sems[3 * i].at[index],
            recv_sem=sems[3 * i + 1].at[index],
            device_id=device(peer),
            device_id_type=MESH,
        )
        copy.start()
        started.append(copy)

    def arrive(i, dst, index, peer):
        pltpu.make_async_remote_copy(
            src_ref=dst,
            dst_ref=dst,
            send_sem=sems[3 * i].at[index],
            recv_sem=sems[3 * i + 1].at[index],
            device_id=device(peer),
            device_id_type=MESH,
        ).wait_recv()

    def keep(i, src, slot):
        copy = pltpu.make_async_copy(src, outs[i].at[slot], sems[3 * i + 2].at[0])
        copy.start()
        locals_.append(copy)

    steps = []
    for i, kind in enumerate(kinds):
        src = ins[i]
        out = outs[i]

        def half(slot, part, out=out):
            rows = out.shape[1] // 2
            if rows < 8:
                return out.at[slot, :, pl.ds(*((0, 256), (256, out.shape[2] - 256))[part])]
            return out.at[slot, pl.ds(part * rows, rows)]

        if kind in ("tag", "hag", "yag"):
            axis = "h" if kind == "hag" else "t"

            def slot_of(j, k, kind=kind):
                if kind == "hag":
                    return at.head(j, 2 * k)
                if kind == "tag":
                    return at.tile(j, k)
                return lax.rem(at.a + j, SIDE)

            def own(part, src=src):
                rows = src.shape[0] // 2
                if rows < 8:
                    return src.at[:, pl.ds(*((0, 256), (256, src.shape[1] - 256))[part])]
                return src.at[pl.ds(part * rows, rows)]

            rest = 18 if kind == "hag" else 20
            gap = 2 if kind == "hag" else 4

            def spread(
                i, k, block=None, axis=axis, slot_of=slot_of, half=half, rest=rest, gap=gap
            ):
                slot = slot_of(0, 4 - k if axis == "t" and k else k)
                for late in (0, 1):
                    for j, first in ((1, 0), (3, 1)):
                        part = first ^ late
                        piece = half(slot, part) if block is None else block(part)
                        index = rest + gap * first + k if late else 4 * j + k
                        send(i, piece, half(slot, part), index, (axis, j, 0))

            def relay(i, k, axis=axis, slot_of=slot_of, half=half):
                back = 4 - k if axis == "t" and k else k
                for j, part in ((1, 0), (3, 1)):
                    piece = half(slot_of(4 - j, back), part)
                    arrive(i, piece, 4 * j + k, (axis, j, 0))
                    send(i, piece, piece, (8 + k, k)[part], (axis, j, 0))

            def settle(i, k, axis=axis, slot_of=slot_of, half=half, out=out, rest=rest, gap=gap, kind=kind):
                back = 4 - k if axis == "t" and k else k
                for j, part in ((1, 0), (3, 1)):
                    slot = slot_of(4 - j, back)
                    arrive(i, half(slot, 1 - part), rest + gap * part + k, (axis, j, 0))
                    if kind == "hag":
                        send(i, out.at[slot], out.at[slot], 4 * j + 2 + k, ("h", 0, 1))

            def far(i, k, axis=axis, slot_of=slot_of, half=half, out=out, kind=kind):
                back = 4 - k if axis == "t" and k else k
                slot = slot_of(2, back)
                arrive(i, half(slot, 0), 8 + k, (axis, 1, 0))
                arrive(i, half(slot, 1), k, (axis, 3, 0))
                if kind == "hag":
                    send(i, out.at[slot], out.at[slot], 10 + k, ("h", 0, 1))

            if kind == "tag":
                for late in (0, 1):
                    for k, first in ((1, 0), (3, 1)):
                        part = first ^ late
                        index = 28 + first if late else 16 + k
                        send(i, own(part), half(at.t, part), index, ("t", 0, k))
                spread(i, 0, own)
                keep(i, src, at.t)

                def onward(i=i, spread=spread, half=half):
                    for k, part in ((1, 0), (3, 1)):
                        piece = half(at.tile(0, 4 - k), part)
                        arrive(i, piece, 16 + k, ("t", 0, k))
                        send(i, piece, piece, (16, 18)[part], ("t", 0, k))
                    for k, part in ((1, 0), (3, 1)):
                        arrive(i, half(at.tile(0, 4 - k), 1 - part), 28 + part, ("t", 0, k))
                        spread(i, k)

                def last(i=i, out=out, spread=spread, half=half):
                    slot = at.tile(0, 2)
                    arrive(i, half(slot, 0), 16, ("t", 0, 1))
                    arrive(i, half(slot, 1), 18, ("t", 0, 3))
                    spread(i, 2)

                steps.append((2, functools.partial(relay, i, 0)))
                steps.append((3, onward))
                steps.append((4.5, functools.partial(relay, i, 1)))
                steps.append((5, last))
                steps.append((5.5, functools.partial(relay, i, 3)))
                steps.append((7, functools.partial(relay, i, 2)))
                for k in (0, 1, 3, 2):
                    steps.append((1000, functools.partial(settle, i, k)))
                    steps.append((1000, functools.partial(far, i, k)))
            elif kind == "hag":
                send(i, src, out.at[at.h], 16, ("h", 0, 2))
                spread(i, 0, own)
                send(i, src, out.at[at.h], 2, ("h", 0, 1))
                keep(i, src, at.h)

                def onward(i=i, out=out, spread=spread):
                    slot = at.head(0, 2)
                    arrive(i, out.at[slot], 16, ("h", 0, 2))
                    spread(i, 1)
                    send(i, out.at[slot], out.at[slot], 3, ("h", 0, 1))

                def finish(i=i, out=out):
                    for k in (0, 1):
                        for j in range(4):
                            slot = at.head(4 - j, 2 * k + 1)
                            arrive(i, out.at[slot], 4 * j + 2 + k, ("h", 0, 1))

                steps.append((1, onward))
                steps.append((1.5, functools.partial(relay, i, 0)))
                steps.append((1.6, functools.partial(settle, i, 0)))
                steps.append((3.2, functools.partial(relay, i, 1)))
                steps.append((4.5, functools.partial(settle, i, 1)))
                steps.append((4, functools.partial(far, i, 0)))
                steps.append((5.2, functools.partial(far, i, 1)))
                steps.append((1001, finish))
            else:
                spread(i, 0, own)
                keep(i, src, at.a)
                steps.append((1, functools.partial(relay, i, 0)))
                steps.append((1000, functools.partial(settle, i, 0)))
                steps.append((1000, functools.partial(far, i, 0)))
        elif kind == "ha2a":
            def give(i=i, src=src, out=out, flips=()):
                for f in flips:
                    for j in range(4):
                        if f or j:
                            send(i, src.at[at.head(j, f)], out.at[at.h], 4 * f + j, ("h", j, f))

            steps.append((3.3, functools.partial(give, flips=(1, 0))))
            keep(i, src.at[at.h], at.h)
            steps.append((5, functools.partial(give, flips=(3, 2))))

            def finish(i=i, out=out):
                for f in range(4):
                    for j in range(4):
                        if f or j:
                            arrive(i, out.at[at.head(4 - j, f)], 4 * f + j, ("h", j, f))

            steps.append((1000, finish))
        elif kind == "ycols":
            width = src.shape[1] // SIDE
            rows = src.shape[0] // 2
            mine = pl.ds(pl.multiple_of(lax.rem(at.h, 2) * rows, rows), rows)
            other = pl.ds(pl.multiple_of((1 - lax.rem(at.h, 2)) * rows, rows), rows)

            def columns(j, width=width):
                return pl.ds(pl.multiple_of(lax.rem(at.a + j, SIDE) * width, 128), width)

            for j in (2, 1, 3):
                send(i, src.at[mine, columns(j)], out.at[at.a, mine], j, ("t", j, 0))
            keep(i, src.at[:, columns(0)], at.a)

            def share(i=i, out=out, mine=mine):
                for j in (1, 3, 2):
                    block = out.at[lax.rem(at.a + 4 - j, SIDE), mine]
                    arrive(i, block, j, ("t", j, 0))
                    send(i, block, block, 4 + j, ("h", 0, 1))

            def finish(i=i, out=out, other=other):
                for j in (1, 3, 2):
                    block = out.at[lax.rem(at.a + 4 - j, SIDE), other]
                    arrive(i, block, 4 + j, ("h", 0, 1))

            steps.append((999, share))
            steps.append((1002, finish))
        else:
            along_z = kind == "zrs"
            held, summed = holds.pop(0), holds.pop(0)

            def spot(j, along_z=along_z):
                return lax.rem((at.b if along_z else at.a) + j, SIDE)

            def peer_of(j, along_z=along_z):
                return ("t", 0, j) if along_z else ("t", j, 0)

            rows = src.shape[1] // 2
            parts = (pl.ds(0, rows), pl.ds(rows, rows))
            for part, j in ((0, 1), (1, 3)):
                send(i, src.at[spot(2), parts[part]], held.at[part], part, peer_of(j))
            for part, j in ((0, 1), (1, 3)):
                rest = parts[1 - part]
                send(i, src.at[spot(j), rest], out.at[1 + part, rest], 2 + part, peer_of(j))
            keep(i, src.at[spot(0)], 0)

            def add(
                i=i, src=src, out=out, held=held, summed=summed, spot=spot, peer_of=peer_of, parts=parts
            ):
                for part, j in ((0, 1), (1, 3)):
                    arrive(i, held.at[part], part, peer_of(j))
                    summed[part] = src[spot(j), parts[part], :] + held[part]
                for part, j in ((0, 1), (1, 3)):
                    send(i, summed.at[part], out.at[1 + part, parts[part]], 4 + part, peer_of(j))

            def finish(i=i, out=out, peer_of=peer_of, parts=parts):
                for part, j in ((0, 1), (1, 3)):
                    arrive(i, out.at[1 + part, parts[1 - part]], 2 + part, peer_of(j))
                    arrive(i, out.at[1 + part, parts[part]], 4 + part, peer_of(j))

            steps.append((2, add))
            steps.append((1000, finish))

    for _, step in sorted(steps, key=lambda step: step[0]):
        step()
    for copy in started:
        copy.wait_send()
    for copy in locals_:
        copy.wait()


def exchange(name, cid, *tasks):
    kinds = tuple(kind for kind, _ in tasks)
    arrays = [array for _, array in tasks]
    shapes = []
    for kind, array in tasks:
        if kind in ("tag", "hag", "yag"):
            piece = array.shape
        elif kind == "ycols":
            piece = (array.shape[0], array.shape[1] // SIDE)
        else:
            piece = array.shape[1:]
        shapes.append(jax.ShapeDtypeStruct((out_slots(kind),) + piece, array.dtype))
    scratch = []
    for kind in kinds:
        scratch += [
            pltpu.SemaphoreType.DMA((TASK_SEMS[kind],)),
            pltpu.SemaphoreType.DMA((TASK_SEMS[kind],)),
            pltpu.SemaphoreType.DMA((1,)),
        ]
    for kind, array in tasks:
        if kind in ("yrs", "zrs"):
            piece = (2, array.shape[1] // 2) + array.shape[2:]
            scratch += [pltpu.VMEM(piece, array.dtype)] * 2
    return pl.pallas_call(
        functools.partial(comm_kernel, kinds),
        out_shape=shapes,
        in_specs=[pl.BlockSpec(memory_space=pltpu.VMEM)] * len(arrays),
        out_specs=[pl.BlockSpec(memory_space=pltpu.VMEM)] * len(arrays),
        scratch_shapes=scratch,
        compiler_params=pltpu.CompilerParams(
            collective_id=cid, has_side_effects=True, vmem_limit_bytes=COMM_LIMIT
        ),
        name=name,
    )(*arrays)


def near(first, second):
    def coords(ids):
        return ids // (TH * TW), ids // TW % TH, ids % TW

    close = True
    for one, two in zip(coords(first), coords(second)):
        close = close & (jnp.abs(one - two) <= 1)
    return close


def attend_kernel(slots_ref, query_ref, kv_ref, att_ref, inv_ref, exp_ref, total_ref, acc_ref):
    mine = slots_ref[lax.axis_index("tile")]
    total_ref[...] = jnp.zeros_like(total_ref)
    acc_ref[...] = jnp.zeros_like(acc_ref)
    count = kv_ref.shape[0]

    @pl.loop(0, count)
    def _(j):
        @pl.when(near(mine, slots_ref[j]))
        def _():
            scores = lax.dot_general(
                query_ref[...], kv_ref[j, :, :HD], NT, preferred_element_type=F32
            )
            grown = jnp.exp(scores * ATT_SCALE)
            exp_ref[j] = grown
            total_ref[...] += jnp.sum(grown, -1, keepdims=True)

    inv = 1.0 / total_ref[...]
    inv_ref[...] = jnp.broadcast_to(inv, inv_ref.shape)

    @pl.loop(0, count)
    def _(j):
        @pl.when(near(mine, slots_ref[j]))
        def _():
            probs = (exp_ref[j] * inv).astype(BF16)
            acc_ref[...] += jnp.dot(probs, kv_ref[j, :, HD:], preferred_element_type=F32)

    att_ref[...] = acc_ref[...].astype(BF16)


def attend(slots, query_b, all_kv):
    rows = query_b.shape[0]
    return pl.pallas_call(
        attend_kernel,
        out_shape=(
            jax.ShapeDtypeStruct((rows, HD), BF16),
            jax.ShapeDtypeStruct((rows, HD), F32),
        ),
        in_specs=[
            pl.BlockSpec(memory_space=pltpu.SMEM),
            pl.BlockSpec(memory_space=pltpu.VMEM),
            pl.BlockSpec(memory_space=pltpu.VMEM),
        ],
        out_specs=(
            pl.BlockSpec(memory_space=pltpu.VMEM),
            pl.BlockSpec(memory_space=pltpu.VMEM),
        ),
        scratch_shapes=[
            pltpu.VMEM((all_kv.shape[0], rows, rows), F32),
            pltpu.VMEM((rows, 1), F32),
            pltpu.VMEM((rows, HD), F32),
        ],
        compiler_params=pltpu.CompilerParams(vmem_limit_bytes=VMEM_LIMIT),
        name="attend",
    )(slots, query_b, all_kv)


def branch_kernel(weight_ref, att_ref, teacher_ref, gate_ref, grad_ref):
    total = None
    for h in range(att_ref.shape[0]):
        term = lax.dot_general(weight_ref[h], att_ref[h], NT, preferred_element_type=F32)
        total = term if total is None else total + term
    gate = gate_ref[...]
    residual = LOSS_WEIGHT * (gate * total - teacher_ref[...].astype(F32))
    grad_ref[...] = (gate * residual).astype(BF16)


def branch_grad(weight_parts, att_parts, teacher_part, gate_part):
    return pl.pallas_call(
        branch_kernel,
        out_shape=jax.ShapeDtypeStruct(teacher_part.shape, BF16),
        in_specs=[pl.BlockSpec(memory_space=pltpu.VMEM)] * 4,
        out_specs=pl.BlockSpec(memory_space=pltpu.VMEM),
        compiler_params=pltpu.CompilerParams(vmem_limit_bytes=VMEM_LIMIT),
        name="branch_grad",
    )(weight_parts, att_parts, teacher_part, gate_part)


def out_kernel(
    grad_ref,
    weight_ref,
    att_ref,
    inv_ref,
    yterm_ref,
    zterm_ref,
    gatt_ref,
    stats_ref,
    delta_ref,
):
    rows = att_ref.shape[0]
    step = grad_ref.shape[1]
    half = step // 2
    grad_t = jnp.zeros((HD, rows), F32)
    for h in range(grad_ref.shape[0]):
        block = grad_ref[h]
        grad_t += jnp.dot(
            weight_ref[:, h * step : (h + 1) * step], block, preferred_element_type=F32
        )
        term = jnp.dot(block, att_ref[...], preferred_element_type=F32)
        low = h % SIDE * half
        yterm_ref[h // SIDE, low : low + half, :] = term[:half]
        low = h // SIDE * half
        zterm_ref[h % SIDE, low : low + half, :] = term[half:]
    gatt = grad_t.T.astype(BF16)
    gatt_ref[...] = gatt
    delta = jnp.sum(gatt.astype(F32) * att_ref[...].astype(F32), -1, keepdims=True)
    delta_all = jnp.broadcast_to(delta, (rows, HD))
    delta_ref[...] = delta_all
    stats_ref[0:4, :] = inv_ref[...].T[0:4]
    stats_ref[4:8, :] = delta_all.T[0:4]


def out_grads(grad_parts, out_weight, attended, inv):
    rows = attended.shape[0]
    parts, step = grad_parts.shape[:2]
    return pl.pallas_call(
        out_kernel,
        out_shape=(
            jax.ShapeDtypeStruct((SIDE, parts // SIDE * step // 2, HD), F32),
            jax.ShapeDtypeStruct((SIDE, parts // SIDE * step // 2, HD), F32),
            jax.ShapeDtypeStruct((rows, HD), BF16),
            jax.ShapeDtypeStruct((8, rows), F32),
            jax.ShapeDtypeStruct((rows, HD), F32),
        ),
        in_specs=[pl.BlockSpec(memory_space=pltpu.VMEM)] * 4,
        out_specs=(pl.BlockSpec(memory_space=pltpu.VMEM),) * 5,
        compiler_params=pltpu.CompilerParams(vmem_limit_bytes=VMEM_LIMIT),
        name="out_grads",
    )(grad_parts, out_weight, attended, inv)


def root_back(grad_unit, values):
    factor = lax.rsqrt(jnp.mean(values * values, -1, keepdims=True) + EPS_ROOT)
    unit = values * factor
    return factor * (grad_unit - unit * jnp.mean(grad_unit * unit, -1, keepdims=True))


def back_kernel(
    slots_ref,
    proj_ref,
    query_ref,
    kv_ref,
    gatt_ref,
    stats_ref,
    inv_ref,
    delta_ref,
    out_ref,
    dq_ref,
    dk_ref,
    dv_ref,
):
    me = lax.axis_index("tile")
    mine = slots_ref[me]
    dq_ref[...] = jnp.zeros_like(dq_ref)
    dk_ref[...] = jnp.zeros_like(dk_ref)
    dv_ref[...] = jnp.zeros_like(dv_ref)
    my_inv = inv_ref[:, 0:1]
    my_delta = delta_ref[:, 0:1]

    @pl.loop(0, kv_ref.shape[0])
    def _(j):
        @pl.when(near(mine, slots_ref[j]))
        def _():
            key_j = kv_ref[j, :, :HD]
            scores = lax.dot_general(query_ref[me], key_j, NT, preferred_element_type=F32)
            probs = jnp.exp(scores * ATT_SCALE) * my_inv
            gprobs = lax.dot_general(
                gatt_ref[me], kv_ref[j, :, HD:], NT, preferred_element_type=F32
            )
            gscores = (probs * (gprobs - my_delta)).astype(BF16)
            dq_ref[...] += jnp.dot(gscores, key_j, preferred_element_type=F32)

            query_j = query_ref[j]
            gatt_j = gatt_ref[j]
            scores_t = lax.dot_general(
                kv_ref[me, :, :HD], query_j, NT, preferred_element_type=F32
            )
            probs_t = jnp.exp(scores_t * ATT_SCALE) * stats_ref[j, 0:1, :]
            dv_ref[...] += jnp.dot(probs_t.astype(BF16), gatt_j, preferred_element_type=F32)
            gprobs_t = lax.dot_general(
                kv_ref[me, :, HD:], gatt_j, NT, preferred_element_type=F32
            )
            gscores_t = (probs_t * (gprobs_t - stats_ref[j, 4:5, :])).astype(BF16)
            dk_ref[...] += jnp.dot(gscores_t, query_j, preferred_element_type=F32)

    out_ref[:, :HD] = root_back(dq_ref[...] * ATT_SCALE, proj_ref[:, :HD]).astype(BF16)
    out_ref[:, HD : 2 * HD] = root_back(
        dk_ref[...] * ATT_SCALE, proj_ref[:, HD : 2 * HD]
    ).astype(BF16)
    out_ref[:, 2 * HD :] = dv_ref[...].astype(BF16)


def attend_back(slots, projected, all_query, all_kv, all_gatt, all_stats, inv, delta):
    rows = projected.shape[0]
    return pl.pallas_call(
        back_kernel,
        out_shape=jax.ShapeDtypeStruct((rows, 3 * HD), BF16),
        in_specs=[pl.BlockSpec(memory_space=pltpu.SMEM)]
        + [pl.BlockSpec(memory_space=pltpu.VMEM)] * 7,
        out_specs=pl.BlockSpec(memory_space=pltpu.VMEM),
        scratch_shapes=[pltpu.VMEM((rows, HD), F32)] * 3,
        compiler_params=pltpu.CompilerParams(vmem_limit_bytes=VMEM_LIMIT),
        name="attend_back",
    )(slots, projected, all_query, all_kv, all_gatt, all_stats, inv, delta)


def terms_kernel(normed_ref, grad_ref, yparts_ref, zparts_ref, qkv_ref, ysum_ref, zsum_ref):
    step = qkv_ref.shape[1]
    for k in range(qkv_ref.shape[0]):
        total = None
        for j in range(normed_ref.shape[0]):
            term = lax.dot_general(
                normed_ref[j, :, k * step : (k + 1) * step],
                grad_ref[j],
                (((0,), (0,)), ((), ())),
                preferred_element_type=F32,
            )
            total = term if total is None else total + term
        qkv_ref[k] = total
    for parts_ref, sum_ref in ((yparts_ref, ysum_ref), (zparts_ref, zsum_ref)):
        half = sum_ref.shape[1]
        for k in range(sum_ref.shape[0]):
            rows = slice(k * half, (k + 1) * half)
            sum_ref[k] = parts_ref[0, rows] + (parts_ref[1, rows] + parts_ref[2, rows])


def grad_terms(normed_parts, qkv_parts, yparts, zparts):
    step = normed_parts.shape[2] // SIDE
    half = yparts.shape[1] // SIDE
    return pl.pallas_call(
        terms_kernel,
        out_shape=(
            jax.ShapeDtypeStruct((SIDE, step, 3 * HD), F32),
            jax.ShapeDtypeStruct((SIDE, half, HD), F32),
            jax.ShapeDtypeStruct((SIDE, half, HD), F32),
        ),
        in_specs=[pl.BlockSpec(memory_space=pltpu.VMEM)] * 4,
        out_specs=(pl.BlockSpec(memory_space=pltpu.VMEM),) * 3,
        compiler_params=pltpu.CompilerParams(vmem_limit_bytes=VMEM_LIMIT),
        name="grad_terms",
    )(normed_parts, qkv_parts, yparts, zparts)


def sums_kernel(qkv_ref, first_ref, second_ref, qkv_out_ref, out_out_ref):
    qkv_out_ref[...] = qkv_ref[0] + (qkv_ref[1] + qkv_ref[2])
    first = first_ref[0] + (first_ref[1] + first_ref[2])
    second = second_ref[0] + (second_ref[1] + second_ref[2])
    half = first.shape[0]
    out_out_ref[:half, :] = first
    out_out_ref[half:, :] = second


def final_sums(qkv_pieces, first, second):
    step = qkv_pieces.shape[1]
    return pl.pallas_call(
        sums_kernel,
        out_shape=(
            jax.ShapeDtypeStruct((step, 3 * HD), F32),
            jax.ShapeDtypeStruct((step, HD), F32),
        ),
        in_specs=[pl.BlockSpec(memory_space=pltpu.VMEM)] * 3,
        out_specs=(pl.BlockSpec(memory_space=pltpu.VMEM),) * 2,
        compiler_params=pltpu.CompilerParams(vmem_limit_bytes=VMEM_LIMIT),
        name="final_sums",
    )(qkv_pieces, first, second)


def modulated_norm(tokens, mod_shift, mod_scale):
    values_in = tokens.astype(F32)
    center = values_in - jnp.mean(values_in, -1, keepdims=True)
    spread = jnp.mean(center * center, -1, keepdims=True)
    return (center * lax.rsqrt(spread + EPS_NORM) * (1.0 + mod_scale) + mod_shift).astype(BF16)


def root_norm(values):
    return values * lax.rsqrt(jnp.mean(values * values, -1, keepdims=True) + EPS_ROOT)


def per_device(tokens, mod_shift, mod_scale, mod_gate, qkv_weight, out_weight, teacher, slot_tiles):
    width = out_weight.shape[1]
    step = width // 16
    head = lax.axis_index("head")
    normed = modulated_norm(tokens, mod_shift, mod_scale)
    projected = jnp.dot(normed, qkv_weight, preferred_element_type=F32)
    query_b = root_norm(projected[:, :HD]).astype(BF16)
    key_b = root_norm(projected[:, HD : 2 * HD]).astype(BF16)
    kv = jnp.concatenate([key_b, projected[:, 2 * HD :].astype(BF16)], 1)
    weight_t = out_weight.T.reshape(16, step, HD)
    teacher_part = lax.dynamic_slice_in_dim(teacher, head * step, step, 1).T
    gate_part = lax.dynamic_slice_in_dim(mod_gate, head * step, step, 0)[:, None]

    (all_kv,) = exchange("share_kv", 1, ("tag", kv))
    attended, inv = attend(slot_tiles, query_b, all_kv)
    att_parts, all_query, weight_parts = exchange(
        "share_att", 2, ("hag", attended), ("tag", query_b), ("ha2a", weight_t)
    )
    grad_part = branch_grad(weight_parts, att_parts, teacher_part, gate_part)
    grad_parts, normed_parts = exchange("share_grad", 3, ("hag", grad_part), ("ycols", normed))
    yterm, zterm, gatt, stats, delta = out_grads(grad_parts, out_weight, attended, inv)
    all_gatt, all_stats = exchange("share_gatt", 4, ("tag", gatt), ("tag", stats))
    grad_qkv = attend_back(
        slot_tiles, projected, all_query, all_kv, all_gatt, all_stats, inv, delta
    )
    qkv_parts, yparts, zparts = exchange(
        "share_qkv", 5, ("yag", grad_qkv), ("yrs", yterm), ("zrs", zterm)
    )
    qkv_term, ysum, zsum = grad_terms(normed_parts, qkv_parts, yparts, zparts)
    qkv_grad, out_grad = final_sums(
        *exchange("share_sums", 6, ("zrs", qkv_term), ("zrs", ysum), ("yrs", zsum))
    )
    return qkv_grad, out_grad.T


def solution(mesh):
    return jax.shard_map(
        per_device,
        mesh=mesh,
        in_specs=(
            P("tile", None),
            P(),
            P(),
            P(),
            P(None, "head"),
            P("head", None),
            P("tile", None),
            P(),
        ),
        out_specs=(P("tile", "head"), P("head", "tile")),
        check_vma=False,
    )
```
